32 devices in a mesh: depth: 8 (over y, x, core), tile: 4 (over z).
Axes of the slice: x: 2, y: 2, z: 4, core: 2. Of those that a mesh axis runs over, the one named last changes fastest.
Arguments:
- concentration: float32 [64, 128, 256], P('depth', 'tile'), may hold values from -6 to 6
- velocity: float32 [3, 64, 128, 256], P(None, 'depth', 'tile'), may hold values from -6 to 6
- diffusivity: float32 [64, 128, 256], P('depth', 'tile'), may hold values from 0.02 to 0.15
Outputs:
- picture: float32 [4, 128, 256], P(None, 'tile', 'depth')
The draws below stay inside these ranges and needn't reach their ends.
All inputs are finite; a program needn't handle non-finite values.
Results may differ from the reference program's by a relative error of at most 0.0003.
Values sent between devices are 32-bit elements; how exact they have to be, the bound alone decides.
A program may use at most 64 MiB of HBM per device.

```python
import math
import jax
import jax.numpy as jnp
from jax import lax

BX = 32
NY = 256
NZ = 64
NX = 128
N_TILE = 4


def level_of(own_key, extent, pieces, low, high):
    loudness, own = 1.0, jax.random.fold_in(own_key, 6)
    for position, blocks in pieces:
        draws = jnp.exp(jax.random.uniform(jax.random.fold_in(own, position), (blocks,), jnp.float32, low / len(pieces), high / len(pieces)))
        loudness = loudness * jnp.repeat(draws, extent[position] // blocks).reshape([-1 if axis == position else 1 for axis in range(len(extent))])
    return loudness


def noise(key, extent, deviation, reach, shards=(), kind=jnp.bfloat16):
    drawn = jax.random.normal(key, extent, jnp.float32) * deviation
    if len(shards) > 0:
        drawn = level_of(key, extent, shards, -0.22, 0.18) * drawn
    return jnp.clip(drawn, min=-reach, max=reach).astype(kind)


def setup_inputs(seed: int = 0) -> dict:
    seeds = jax.random.split(jax.random.key(seed), 4)
    concentration = noise(seeds[0], (NZ, NX, NY), 1.0, 6.0, ((0, 8), (1, 4)), jnp.float32)
    velocity = noise(seeds[1], (3, NZ, NX, NY), 1.0, 6.0, ((1, 8), (2, 4)), jnp.float32)
    diffusivity = jnp.clip(jnp.exp(math.log(0.15) - 2.014903 * jax.random.uniform(seeds[2], (NZ, NX, NY), jnp.float32) ** level_of(seeds[2], (NZ, NX, NY), ((0, 8), (1, 4)), -0.2, 0.2)), 0.02, 0.15)
    return dict(concentration=concentration, velocity=velocity, diffusivity=diffusivity)


ADVECT = 0.25

def update(padded, velocity, diffusion):
    center = padded[1:-1, 1:-1, 1:-1]
    front_cells = padded[2:, 1:-1, 1:-1]
    back_cells = padded[:-2, 1:-1, 1:-1]
    right_cells = padded[1:-1, 2:, 1:-1]
    left_cells = padded[1:-1, :-2, 1:-1]
    upper_cells = padded[1:-1, 1:-1, 2:]
    lower_cells = padded[1:-1, 1:-1, :-2]
    laplace = front_cells + back_cells + right_cells + left_cells + upper_cells + lower_cells - 6.0 * center
    advect = velocity[0] * (front_cells - back_cells) + velocity[1] * (right_cells - left_cells) + velocity[2] * (upper_cells - lower_cells)
    return center + diffusion * laplace - 0.5 * ADVECT * advect

def emission(mixed_field, bright):
    return jnp.stack([mixed_field, jnp.tanh(mixed_field), mixed_field * mixed_field - 1.0], 0) * bright

def opacity(mixed_field, depth_total):
    return 2.0 / depth_total * (0.5 + jax.nn.sigmoid(2.0 * mixed_field))

def reference(concentration, velocity, diffusivity):
    bright = math.sqrt(NZ)
    padded = jnp.pad(concentration, 1)

    def one_block(block_index):
        offset = (block_index * BX).astype(jnp.int32)
        slab_rows = lax.dynamic_slice_in_dim(padded, offset, BX + 2, 1)
        flow = lax.dynamic_slice_in_dim(velocity, offset, BX, 2)
        spread_rate = lax.dynamic_slice_in_dim(diffusivity, offset, BX, 1)
        mixed_field = update(slab_rows, flow, spread_rate)
        optical = opacity(mixed_field, NZ)
        before = jnp.cumsum(optical, axis=0) - optical
        weight = jnp.exp(-before) * (1.0 - jnp.exp(-optical))
        colors = lax.optimization_barrier(jnp.sum(weight[None] * emission(mixed_field, bright), axis=1))
        coverage = 1.0 - jnp.exp(-lax.optimization_barrier(jnp.sum(optical, axis=0)))
        return jnp.concatenate([colors, coverage[None]], 0)
    blocks = lax.map(one_block, jnp.arange(N_TILE, dtype=jnp.int32))
    return jnp.transpose(blocks, (1, 0, 2, 3)).reshape(4, NX, NY)
```

```python
import functools
import math

import jax
import jax.numpy as jnp
from jax import lax
from jax.experimental import pallas as pl
from jax.experimental.pallas import tpu as pltpu
from jax.sharding import PartitionSpec as P

ADVECT = 0.25
LANES = 128
ROWS = 8
SLOT = LANES // 4
VALUES = 11
MESH = pl.DeviceIdType.MESH


def transpose_slots(tiles):
    slot = lax.broadcasted_iota(jnp.int32, (ROWS, LANES), 1) // SLOT
    a, b, c, d = tiles
    odd, high = slot % 2 == 1, slot >= 2

    def swap(x, y, step, mask):
        return (
            jnp.where(mask, pltpu.roll(y, step, 1), x),
            jnp.where(mask, y, pltpu.roll(x, LANES - step, 1)),
        )

    a, b = swap(a, b, SLOT, odd)
    c, d = swap(c, d, SLOT, odd)
    a, c = swap(a, c, 2 * SLOT, high)
    b, d = swap(b, d, 2 * SLOT, high)
    return a, b, c, d


def kernel(
    n,
    tiles,
    conc_hbm,
    vel_hbm,
    diff_hbm,
    out_ref,
    conc,
    vel,
    diff,
    values,
    edges,
    x_edge,
    x_left,
    x_right,
    send,
    recv,
    load_sem,
    edge_send,
    edge_recv,
    part_send,
    part_recv,
):
    layers, width, rays = diff.shape
    groups = width // ROWS
    own = rays // n
    total = layers * n
    half = 0.5 * ADVECT
    bright = math.sqrt(total)
    me = lax.axis_index("depth")
    lane_block = lax.axis_index("tile")
    left, right = lane_block == 0, lane_block == tiles - 1

    load_conc = pltpu.make_async_copy(
        conc_hbm, conc.at[:, pl.ds(ROWS, width), :], load_sem.at[0]
    )
    load_conc.start()
    load_vel = pltpu.make_async_copy(vel_hbm, vel, load_sem.at[1])
    load_vel.start()
    load_diff = pltpu.make_async_copy(diff_hbm, diff, load_sem.at[2])
    load_diff.start()

    barrier = pltpu.get_barrier_semaphore()
    for k in range(1, n):
        pl.semaphore_signal(
            barrier, inc=1, device_id={"depth": lax.rem(me + k, n)}, device_id_type=MESH
        )

    @pl.when(jnp.logical_not(left))
    def _():
        for k in range(n):
            pl.semaphore_signal(
                barrier, inc=1, device_id=(k, lax.rem(lane_block + tiles - 1, tiles)), device_id_type=MESH
            )

    @pl.when(jnp.logical_not(right))
    def _():
        for k in range(n):
            pl.semaphore_signal(
                barrier, inc=1, device_id=(k, lax.rem(lane_block + 1, tiles)), device_id_type=MESH
            )

    zero_rows = jnp.zeros((ROWS, rays), jnp.float32)
    for z in range(layers):
        conc[z, pl.ds(0, ROWS), :] = zero_rows
        conc[z, pl.ds(ROWS + width, ROWS), :] = zero_rows

    @pl.when(left)
    def _():
        x_left[...] = jnp.zeros_like(x_left)

    @pl.when(right)
    def _():
        x_right[...] = jnp.zeros_like(x_right)

    load_conc.wait()
    for z in range(layers):
        x_edge[0, pl.ds(z, 1), :] = conc[z, pl.ds(ROWS, 1), :]
        x_edge[1, pl.ds(z, 1), :] = conc[z, pl.ds(ROWS + width - 1, 1), :]

    def to_right(k):
        return pltpu.make_async_remote_copy(
            src_ref=x_edge.at[1, :, pl.ds(k * own // LANES * LANES, LANES)],
            dst_ref=x_left.at[me],
            send_sem=edge_send.at[0, k],
            recv_sem=edge_recv.at[0, me],
            device_id=(k, lax.rem(lane_block + 1, tiles)),
            device_id_type=MESH,
        )

    def to_left(k):
        return pltpu.make_async_remote_copy(
            src_ref=x_edge.at[0, :, pl.ds(k * own // LANES * LANES, LANES)],
            dst_ref=x_right.at[me],
            send_sem=edge_send.at[1, k],
            recv_sem=edge_recv.at[1, me],
            device_id=(k, lax.rem(lane_block + tiles - 1, tiles)),
            device_id_type=MESH,
        )

    def from_tile(side, s):
        return pltpu.make_async_remote_copy(
            src_ref=x_edge.at[side, :, pl.ds(0, LANES)],
            dst_ref=(x_left, x_right)[side].at[s],
            send_sem=edge_send.at[side, s],
            recv_sem=edge_recv.at[side, s],
            device_id=(s, lax.rem(lane_block + 1, tiles)),
            device_id_type=MESH,
        )

    beside = jnp.where(left, 0, 1) + jnp.where(right, 0, 1)
    pl.semaphore_wait(barrier, n - 1 + n * beside)

    @pl.when(jnp.logical_not(left))
    def _():
        for k in range(n):
            to_left(k).start()

    @pl.when(jnp.logical_not(right))
    def _():
        for k in range(n):
            to_right(k).start()

    load_vel.wait()
    load_diff.wait()

    lane = lax.broadcasted_iota(jnp.int32, (ROWS, rays), 1)

    def local_update(z, start):
        rows = pl.ds(start, ROWS)
        here = conc[z, pl.ds(ROWS + start, ROWS), :]
        left_cells = conc[z, pl.ds(ROWS + start - 1, ROWS), :]
        right_cells = conc[z, pl.ds(ROWS + start + 1, ROWS), :]
        lower_cells = jnp.where(lane == 0, 0.0, pltpu.roll(here, 1, 1))
        upper_cells = jnp.where(lane == rays - 1, 0.0, pltpu.roll(here, rays - 1, 1))
        spread = left_cells + right_cells + lower_cells + upper_cells
        flow = vel[1, z, rows, :] * (right_cells - left_cells) + vel[2, z, rows, :] * (
            upper_cells - lower_cells
        )
        if z > 0:
            back = conc[z - 1, pl.ds(ROWS + start, ROWS), :]
            spread = spread + back
        if z < layers - 1:
            front = conc[z + 1, pl.ds(ROWS + start, ROWS), :]
            spread = spread + front
        if 0 < z < layers - 1:
            slope = front - back
        elif z > 0:
            slope = -back
        else:
            slope = front
        flow = flow + vel[0, z, rows, :] * slope
        return here + diff[z, rows, :] * (spread - 6.0 * here) - half * flow

    def shade(mixed):
        bend = jnp.tanh(mixed)
        passed = jnp.exp((bend + 2.0) * (-1.0 / total))
        return bend, passed

    def add_cell(state, mixed):
        bend, passed = shade(mixed)
        if state is None:
            weight = 1.0 - passed
            return weight * mixed, weight * bend, weight * (mixed * mixed - 1.0), passed
        one, two, three, through = state
        weight = through * (1.0 - passed)
        return (
            one + weight * mixed,
            two + weight * bend,
            three + weight * (mixed * mixed - 1.0),
            through * passed,
        )

    for g in range(groups):
        start = g * ROWS
        rows = pl.ds(start, ROWS)
        state = None
        for z in range(layers):
            mixed = local_update(z, start)
            if z == 0:
                values[0, rows, :] = mixed
                values[1, rows, :] = diff[z, rows, :] + half * vel[0, z, rows, :]
                values[2, rows, :] = conc[z, pl.ds(ROWS + start, ROWS), :]
            elif z == layers - 1:
                values[3, rows, :] = mixed
                values[4, rows, :] = diff[z, rows, :] - half * vel[0, z, rows, :]
                values[5, rows, :] = conc[z, pl.ds(ROWS + start, ROWS), :]
            else:
                state = add_cell(state, mixed)
            if g == 0:
                edges[0, pl.ds(z, 1), :] = mixed[:1]
                gain = diff[z, rows, :] + half * vel[1, z, rows, :]
                edges[2, pl.ds(z, 1), :] = gain[:1]
            if g == groups - 1:
                edges[1, pl.ds(z, 1), :] = mixed[ROWS - 1 :]
                gain = diff[z, rows, :] - half * vel[1, z, rows, :]
                edges[3, pl.ds(z, 1), :] = gain[ROWS - 1 :]
        for c in range(4):
            values[6 + c, rows, :] = state[c]

    slot_of = lax.broadcasted_iota(jnp.int32, (ROWS, LANES), 1) // SLOT

    def pieces(v, tile):
        lanes = pl.ds(tile * LANES, LANES)
        if v == VALUES - 1:
            return [edges[i, :, lanes] for i in range(4)]
        return [values[v, pl.ds(g * ROWS, ROWS), lanes] for g in range(groups)]

    def pack(tile):
        held = LANES // own
        for v in range(VALUES):
            source = pieces(v, tile)
            if own == SLOT and len(source) == 4:
                for j, block in enumerate(transpose_slots(source)):
                    send[tile * held + j, v] = block
            else:
                for j in range(held):
                    block = None
                    for g, piece in enumerate(source):
                        shift = (SLOT * g - j * own) % LANES
                        if shift:
                            piece = pltpu.roll(piece, shift, 1)
                        block = piece if block is None else jnp.where(slot_of == g, piece, block)
                    send[tile * held + j, v] = block

    def part(target, k):
        return pltpu.make_async_remote_copy(
            src_ref=send.at[target],
            dst_ref=recv.at[k],
            send_sem=part_send.at[k],
            recv_sem=part_recv.at[k],
            device_id={"depth": target},
            device_id_type=MESH,
        )

    for tile in range(rays // LANES):
        pack(tile)
    early = 2
    for d in range(early):

        @pl.when(me != d)
        def _():
            part(d, lax.rem(d - me + n, n)).start()

    for k in range(1, n):
        target = lax.rem(me + k, n)

        @pl.when(target >= early)
        def _():
            part(target, k).start()

    recv[0] = send[me]

    for side, absent in ((0, left), (1, right)):

        @pl.when(jnp.logical_not(absent))
        def _():
            for s in range(n):
                from_tile(side, s).wait_recv()

    for k in range(1, n):
        part(me, k).wait_recv()

    sub = lax.broadcasted_iota(jnp.int32, (ROWS, LANES), 0)
    offset = lax.rem(me * own, LANES)
    index = [lax.rem(me - s + n, n) for s in range(n)]
    state = None
    edge_cells = []
    for s in range(n):
        p0, a0, p7, b7 = (recv[index[s], v] for v in (0, 1, 3, 4))
        zero = jnp.zeros((ROWS, LANES), jnp.float32)
        f0 = a0 * recv[index[s - 1], 5] if s > 0 else zero
        f7 = b7 * recv[index[s + 1], 2] if s < n - 1 else zero
        state = add_cell(state, p0 + f0)
        through = state[3]
        state = tuple(state[c] + through * recv[index[s], 6 + c] for c in range(3)) + (
            through * recv[index[s], 9],
        )
        state = add_cell(state, p7 + f7)
        swing = LANES - (groups - 2) * SLOT
        f0_last = pltpu.roll(pltpu.roll(f0, swing, 1), 1, 0)
        f7_last = pltpu.roll(f7, swing, 1)
        f7_first = pltpu.roll(f7, ROWS - 1, 0)
        outer = jnp.where(
            sub == 0,
            jnp.where(slot_of == 0, f0, f0_last),
            jnp.where(sub == ROWS - 1, jnp.where(slot_of == 0, f7_first, f7_last), 0.0),
        )
        packed = recv[index[s], VALUES - 1]
        beside_cells = jnp.where(
            slot_of == 0,
            pltpu.roll(x_left[s], lax.rem(LANES - offset, LANES), 1),
            pltpu.roll(x_right[s], lax.rem(LANES + SLOT - offset, LANES), 1),
        )
        edge_cells.append(packed + pltpu.roll(packed, LANES // 2, 1) * beside_cells + outer)

    picture = [bright * state[c] for c in range(3)] + [1.0 - state[3]]

    through = None
    sums = None
    for s in range(0, n, 2):
        mixed = jnp.where(slot_of < 2, edge_cells[s], pltpu.roll(edge_cells[s + 1], LANES // 2, 1))
        bend, passed = shade(mixed)
        scan = passed
        for step in (1, 2, 4):
            scan = scan * jnp.where(sub >= step, pltpu.roll(scan, step, 0), 1.0)
        before = jnp.where(sub >= 1, pltpu.roll(scan, 1, 0), 1.0)
        both = jnp.broadcast_to(scan[ROWS - 1 :], (ROWS, LANES))
        other = pltpu.roll(both, LANES // 2, 1)
        before = before * jnp.where(slot_of < 2, 1.0, other)
        if through is not None:
            before = before * through
        weight = before * (1.0 - passed)
        terms = (weight * mixed, weight * bend, weight * (mixed * mixed - 1.0))
        sums = terms if sums is None else tuple(x + y for x, y in zip(sums, terms))
        through = both * other if through is None else through * (both * other)
    edge_rows = []
    for c in range(3):
        x = sums[c] + pltpu.roll(sums[c], LANES // 2, 1)
        edge_rows.append(bright * jnp.sum(x, axis=0, keepdims=True))
    edge_rows.append(1.0 - through[:1])

    for c in range(4):
        for g in range(groups):
            color = pltpu.roll(picture[c], LANES - SLOT * g, 1) if g else picture[c]
            out_ref[c, pl.ds(g * ROWS, ROWS), :] = color[:, :own]
        out_ref[c, pl.ds(0, 1), :] = edge_rows[c][:, :own]
        out_ref[c, pl.ds(width - 1, 1), :] = pltpu.roll(edge_rows[c], LANES - SLOT, 1)[:, :own]

    @pl.when(jnp.logical_not(left))
    def _():
        for k in range(n):
            to_left(k).wait_send()

    @pl.when(jnp.logical_not(right))
    def _():
        for k in range(n):
            to_right(k).wait_send()

    for k in range(1, n):
        part(me, k).wait_send()


def solution(mesh):
    n, tiles = mesh.shape["depth"], mesh.shape["tile"]

    def body(concentration, velocity, diffusivity):
        layers, width, rays = concentration.shape
        groups = width // ROWS
        own = rays // n
        assert own <= SLOT and LANES % own == 0 and layers == ROWS and groups == 4 and n % 2 == 0
        scratch = [
            pltpu.VMEM((layers, width + 2 * ROWS, rays), jnp.float32),
            pltpu.VMEM(velocity.shape, jnp.float32),
            pltpu.VMEM(diffusivity.shape, jnp.float32),
            pltpu.VMEM((VALUES - 1, width, rays), jnp.float32),
            pltpu.VMEM((4, layers, rays), jnp.float32),
            pltpu.VMEM((2, layers, rays), jnp.float32),
            pltpu.VMEM((n, layers, LANES), jnp.float32),
            pltpu.VMEM((n, layers, LANES), jnp.float32),
            pltpu.VMEM((n, VALUES, ROWS, LANES), jnp.float32),
            pltpu.VMEM((n, VALUES, ROWS, LANES), jnp.float32),
            pltpu.SemaphoreType.DMA((3,)),
            pltpu.SemaphoreType.DMA((2, n)),
            pltpu.SemaphoreType.DMA((2, n)),
            pltpu.SemaphoreType.DMA((n,)),
            pltpu.SemaphoreType.DMA((n,)),
        ]
        return pl.pallas_call(
            functools.partial(kernel, n, tiles),
            out_shape=jax.ShapeDtypeStruct((4, width, own), jnp.float32),
            in_specs=[pl.BlockSpec(memory_space=pl.ANY)] * 3,
            out_specs=pl.BlockSpec(memory_space=pltpu.VMEM),
            scratch_shapes=scratch,
            compiler_params=pltpu.CompilerParams(collective_id=0, has_side_effects=True, vmem_limit_bytes=16 << 20),
        )(*[pltpu.with_memory_space_constraint(v, pltpu.HBM) for v in (concentration, velocity, diffusivity)])

    return jax.shard_map(
        body,
        mesh=mesh,
        in_specs=(
            P("depth", "tile", None),
            P(None, "depth", "tile", None),
            P("depth", "tile", None),
        ),
        out_specs=P(None, "tile", "depth"),
        check_vma=False,
    )
```

```python
import functools
import math

import jax
import jax.numpy as jnp
from jax import lax
from jax.experimental import pallas as pl
from jax.experimental.pallas import tpu as pltpu
from jax.sharding import PartitionSpec as P

ADVECT = 0.25
LANES = 128
ROWS = 8
SLOT = LANES // 4
MESH = pl.DeviceIdType.MESH


def transpose_slots(tiles):
    slot = lax.broadcasted_iota(jnp.int32, (ROWS, LANES), 1) // SLOT
    a, b, c, d = tiles
    odd, high = slot % 2 == 1, slot >= 2

    def swap(x, y, step, mask):
        return (
            jnp.where(mask, pltpu.roll(y, step, 1), x),
            jnp.where(mask, y, pltpu.roll(x, LANES - step, 1)),
        )

    a, b = swap(a, b, SLOT, odd)
    c, d = swap(c, d, SLOT, odd)
    a, c = swap(a, c, 2 * SLOT, high)
    b, d = swap(b, d, 2 * SLOT, high)
    return a, b, c, d


def kernel(
    n,
    tiles,
    conc_hbm,
    vel_hbm,
    diff_hbm,
    out_ref,
    conc,
    vel,
    diff,
    values,
    edges,
    x_rows,
    x_send,
    x_recv,
    z_send,
    z_recv,
    held,
    held_edge,
    send_outer,
    recv_outer,
    send_inner,
    recv_inner,
    ready,
    load_sem,
    z_sem,
    x_send_sem,
    x_recv_sem,
    outer_sem,
    inner_sem,
):
    layers, width, rays = diff.shape
    groups = width // ROWS
    own = rays // n
    per_tile = LANES // own
    total = layers * n
    half = 0.5 * ADVECT
    bright = math.sqrt(total)
    me = lax.axis_index("depth")
    lane_block = lax.axis_index("tile")
    left, right = lane_block == 0, lane_block == tiles - 1
    before_tile = lax.rem(lane_block + tiles - 1, tiles)
    after_tile = lax.rem(lane_block + 1, tiles)
    parity = lax.rem(me, 2)
    odd = parity == 1
    sibling = me + 1 - 2 * parity
    z_outer = parity * (layers - 1)
    z_inner = (1 - parity) * (layers - 1)

    load_conc = pltpu.make_async_copy(
        conc_hbm, conc.at[:, pl.ds(ROWS, width), :], load_sem.at[0]
    )
    load_conc.start()
    load_vel = pltpu.make_async_copy(vel_hbm, vel, load_sem.at[1])
    load_vel.start()
    load_diff = pltpu.make_async_copy(diff_hbm, diff, load_sem.at[2])
    load_diff.start()
    x_recv[...] = jnp.zeros_like(x_recv)

    barrier = pltpu.get_barrier_semaphore()
    for k in range(1, n):
        pl.semaphore_signal(
            barrier, inc=1, device_id={"depth": lax.rem(me + k, n)}, device_id_type=MESH
        )

    @pl.when(jnp.logical_not(left))
    def _():
        pl.semaphore_signal(barrier, inc=1, device_id=(me, before_tile), device_id_type=MESH)

    @pl.when(jnp.logical_not(right))
    def _():
        pl.semaphore_signal(barrier, inc=1, device_id=(me, after_tile), device_id_type=MESH)

    zero_rows = jnp.zeros((ROWS, rays), jnp.float32)
    for z in range(layers):
        conc[z, pl.ds(0, ROWS), :] = zero_rows
        conc[z, pl.ds(ROWS + width, ROWS), :] = zero_rows
    x_rows[...] = jnp.zeros_like(x_rows)

    slot_of = lax.broadcasted_iota(jnp.int32, (ROWS, LANES), 1) // SLOT
    sub = lax.broadcasted_iota(jnp.int32, (ROWS, LANES), 0)

    def pack(piece, store):
        for tile in range(rays // LANES):
            source = [piece(g, pl.ds(tile * LANES, LANES)) for g in range(4)]
            if own == SLOT:
                for j, block in enumerate(transpose_slots(source)):
                    store(tile * per_tile + j, block)
                continue
            for j in range(per_tile):
                block = None
                for g in range(4):
                    shift = (SLOT * g - j * own) % LANES
                    moved = pltpu.roll(source[g], shift, 1) if shift else source[g]
                    block = moved if block is None else jnp.where(slot_of == g, moved, block)
                store(tile * per_tile + j, block)

    def into(ref, *where):
        def store(k, block):
            ref[(k, *where)] = block

        return store

    load_conc.wait()
    pack(lambda g, lanes: conc[z_inner, pl.ds(ROWS + g * ROWS, ROWS), lanes], into(z_send))

    z_copy = pltpu.make_async_remote_copy(
        src_ref=z_send,
        dst_ref=z_recv,
        send_sem=z_sem.at[0],
        recv_sem=z_sem.at[1],
        device_id={"depth": sibling},
        device_id_type=MESH,
    )
    beside = jnp.where(left, 0, 1) + jnp.where(right, 0, 1)
    pl.semaphore_wait(barrier, n - 1 + beside)
    z_copy.start()

    @pl.when(jnp.logical_not(left))
    def _():
        pl.semaphore_signal(ready.at[1], inc=1, device_id=(me, before_tile), device_id_type=MESH)

    @pl.when(jnp.logical_not(right))
    def _():
        pl.semaphore_signal(ready.at[0], inc=1, device_id=(me, after_tile), device_id_type=MESH)

    for z in range(layers):
        q, r = z % 4, z // 4
        x_rows[q, pl.ds(r, 1), :] = conc[z, pl.ds(ROWS, 1), :]
        x_rows[q, pl.ds(2 + r, 1), :] = conc[z, pl.ds(ROWS + width - 1, 1), :]
    pack(lambda g, lanes: x_rows[g, :, lanes], into(x_send))
    pack(lambda g, lanes: conc[z_outer, pl.ds(ROWS + g * ROWS, ROWS), lanes], into(send_outer, 2))

    load_vel.wait()
    load_diff.wait()

    lane = lax.broadcasted_iota(jnp.int32, (ROWS, rays), 1)

    def local_update(z, start):
        rows = pl.ds(start, ROWS)
        here = conc[z, pl.ds(ROWS + start, ROWS), :]
        left_cells = conc[z, pl.ds(ROWS + start - 1, ROWS), :]
        right_cells = conc[z, pl.ds(ROWS + start + 1, ROWS), :]
        lower_cells = jnp.where(lane == 0, 0.0, pltpu.roll(here, 1, 1))
        upper_cells = jnp.where(lane == rays - 1, 0.0, pltpu.roll(here, rays - 1, 1))
        spread = left_cells + right_cells + lower_cells + upper_cells
        flow = vel[1, z, rows, :] * (right_cells - left_cells) + vel[2, z, rows, :] * (
            upper_cells - lower_cells
        )
        if z > 0:
            back = conc[z - 1, pl.ds(ROWS + start, ROWS), :]
            spread = spread + back
        if z < layers - 1:
            front = conc[z + 1, pl.ds(ROWS + start, ROWS), :]
            spread = spread + front
        if 0 < z < layers - 1:
            slope = front - back
        elif z > 0:
            slope = -back
        else:
            slope = front
        flow = flow + vel[0, z, rows, :] * slope
        return here + diff[z, rows, :] * (spread - 6.0 * here) - half * flow

    def shade(mixed):
        bend = jnp.tanh(mixed)
        passed = jnp.exp((bend + 2.0) * (-1.0 / total))
        return bend, passed

    def add_cell(state, mixed):
        bend, passed = shade(mixed)
        if state is None:
            weight = 1.0 - passed
            return weight * mixed, weight * bend, weight * (mixed * mixed - 1.0), passed
        one, two, three, through = state
        weight = through * (1.0 - passed)
        return (
            one + weight * mixed,
            two + weight * bend,
            three + weight * (mixed * mixed - 1.0),
            through * passed,
        )

    def note_edge(z, g, mixed):
        rows = pl.ds(g * ROWS, ROWS)
        q, r = z % 4, z // 4
        if g == 0:
            gain = diff[z, rows, :] + half * vel[1, z, rows, :]
            edges[q, pl.ds(r, 1), :] = mixed[:1]
            edges[q, pl.ds(4 + r, 1), :] = gain[:1]
        if g == groups - 1:
            gain = diff[z, rows, :] - half * vel[1, z, rows, :]
            edges[q, pl.ds(2 + r, 1), :] = mixed[ROWS - 1 :]
            edges[q, pl.ds(6 + r, 1), :] = gain[ROWS - 1 :]

    for g in range(groups):
        rows = pl.ds(g * ROWS, ROWS)
        pair = []
        for z, sign in ((0, half), (layers - 1, -half)):
            mixed = local_update(z, g * ROWS)
            note_edge(z, g, mixed)
            pair.append((mixed, diff[z, rows, :] + sign * vel[0, z, rows, :]))
        for i in range(2):
            values[i, rows, :] = jnp.where(odd, pair[1][i], pair[0][i])
            values[2 + i, rows, :] = jnp.where(odd, pair[0][i], pair[1][i])

    def piece_of(v):
        return lambda g, lanes: values[v, pl.ds(g * ROWS, ROWS), lanes]

    for i in range(2):
        pack(piece_of(i), into(send_outer, i))

    def outer(target, k):
        return pltpu.make_async_remote_copy(
            src_ref=send_outer.at[target],
            dst_ref=recv_outer.at[k],
            send_sem=outer_sem.at[0],
            recv_sem=outer_sem.at[1],
            device_id={"depth": target},
            device_id_type=MESH,
        )

    def inner(target, k):
        return pltpu.make_async_remote_copy(
            src_ref=send_inner.at[target],
            dst_ref=recv_inner.at[k],
            send_sem=inner_sem.at[0],
            recv_sem=inner_sem.at[1],
            device_id={"depth": target},
            device_id_type=MESH,
        )

    for k in range(1, n):
        outer(lax.rem(me + k, n), k).start()
    recv_outer[0] = send_outer[me]

    for g in range(groups):
        rows = pl.ds(g * ROWS, ROWS)
        state = None
        for z in range(1, layers - 1):
            mixed = local_update(z, g * ROWS)
            note_edge(z, g, mixed)
            state = add_cell(state, mixed)
        for c in range(4):
            values[4 + c, rows, :] = state[c]
    for v in range(6):
        pack(piece_of(2 + v), into(held, v))
    pack(lambda g, lanes: edges[g, :, lanes], into(held_edge))

    def into_edges(change, z):
        if z == 0:
            first, last = change, pltpu.roll(pltpu.roll(change, SLOT, 1), 3, 0)
            where = slot_of == 0, sub == 0, sub == 2
        else:
            first = pltpu.roll(pltpu.roll(change, LANES - SLOT, 1), 1, 0)
            last = pltpu.roll(change, 4, 0)
            where = slot_of == 3, sub == 1, sub == 3
        moved = jnp.where(where[1], first, jnp.where(where[2], last, 0.0))
        return jnp.where(where[0], moved, 0.0)

    z_copy.wait_recv()
    for k in range(n):
        change = held[k, 1] * z_recv[k]
        mixed = held[k, 0] + change
        bend, passed = shade(mixed)
        through = held[k, 5]
        weight = 1.0 - passed
        scale = jnp.where(odd, passed, 1.0)
        weight = jnp.where(odd, weight, weight * through)
        for c, term in enumerate((mixed, bend, mixed * mixed - 1.0)):
            send_inner[k, c] = scale * held[k, 2 + c] + weight * term
        send_inner[k, 3] = through * passed
        send_inner[k, 4] = held_edge[k] + jnp.where(
            odd, into_edges(change, 0), into_edges(change, layers - 1)
        )
    for k in range(1, n):
        inner(lax.rem(me + k, n), k).start()

    def to_left(k):
        return pltpu.make_async_remote_copy(
            src_ref=x_send.at[k, pl.ds(0, 2)],
            dst_ref=x_recv.at[me, pl.ds(2, 2)],
            send_sem=x_send_sem.at[0],
            recv_sem=x_recv_sem.at[1],
            device_id=(k, before_tile),
            device_id_type=MESH,
        )

    def to_right(k):
        return pltpu.make_async_remote_copy(
            src_ref=x_send.at[k, pl.ds(2, 2)],
            dst_ref=x_recv.at[me, pl.ds(0, 2)],
            send_sem=x_send_sem.at[1],
            recv_sem=x_recv_sem.at[0],
            device_id=(k, after_tile),
            device_id_type=MESH,
        )

    @pl.when(jnp.logical_not(left))
    def _():
        pl.semaphore_wait(ready.at[0], 1)
        for k in range(n):
            to_left(k).start()

    @pl.when(jnp.logical_not(right))
    def _():
        pl.semaphore_wait(ready.at[1], 1)
        for k in range(n):
            to_right(k).start()

    recv_inner[0] = send_inner[me]

    def all_of(send, recv, sems):
        rest = pl.ds(1, n - 1)
        return pltpu.make_async_remote_copy(
            src_ref=send.at[rest],
            dst_ref=recv.at[rest],
            send_sem=sems.at[0],
            recv_sem=sems.at[1],
            device_id={"depth": sibling},
            device_id_type=MESH,
        )

    def all_edges(side):
        return pltpu.make_async_remote_copy(
            src_ref=x_send.at[:, pl.ds(2 * side, 2)],
            dst_ref=x_recv.at[:, pl.ds(2 * side, 2)],
            send_sem=x_send_sem.at[side],
            recv_sem=x_recv_sem.at[side],
            device_id={"depth": sibling},
            device_id_type=MESH,
        )

    outer_copies = all_of(send_outer, recv_outer, outer_sem)
    inner_copies = all_of(send_inner, recv_inner, inner_sem)

    outer_copies.wait_recv()
    index = [lax.rem(me - s + n, n) for s in range(n)]
    cells = []
    edge_cells = []
    for s in range(n):
        beyond = s - 1 if s % 2 == 0 else s + 1
        mixed = recv_outer[index[s], 0]
        change = None
        if 0 <= beyond < n:
            change = recv_outer[index[s], 1] * recv_outer[index[beyond], 2]
            mixed = mixed + change
            change = into_edges(change, 0 if s % 2 == 0 else layers - 1)
        bend, passed = shade(mixed)
        cells.append((mixed, bend, mixed * mixed - 1.0, passed))
        edge_cells.append(change)

    inner_copies.wait_recv()
    state = None
    for s in range(n):
        bricks = [None, None]
        *terms, passed = cells[s]
        weight = 1.0 - passed
        bricks[s % 2] = tuple(weight * x for x in terms) + (passed,)
        bricks[1 - s % 2] = tuple(recv_inner[index[s], c] for c in range(4))
        for brick in bricks:
            if state is None:
                state = brick
            else:
                through = state[3]
                state = tuple(state[c] + through * brick[c] for c in range(3)) + (
                    through * brick[3],
                )
    picture = [bright * state[c] for c in range(3)] + [1.0 - state[3]]
    for c in range(4):
        for g in range(groups):
            color = pltpu.roll(picture[c], LANES - SLOT * g, 1) if g else picture[c]
            out_ref[c, pl.ds(g * ROWS, ROWS), :] = color[:, :own]

    for side, absent in ((0, left), (1, right)):

        @pl.when(jnp.logical_not(absent))
        def _():
            all_edges(side).wait_recv()

    through = None
    sums = None
    odd_row, low = sub % 2 == 1, sub < 4
    for s in range(0, n, 2):
        two = []
        for i in (s, s + 1):
            packed = recv_inner[index[i], 4]
            mixed = packed + pltpu.roll(packed, 4, 0) * x_recv[i]
            two.append(mixed if edge_cells[i] is None else mixed + edge_cells[i])
        mixed = jnp.where(low, two[0], pltpu.roll(two[1], 4, 0))
        bend, passed = shade(mixed)
        scan = passed * jnp.where(slot_of >= 1, pltpu.roll(passed, SLOT, 1), 1.0)
        scan = scan * jnp.where(slot_of >= 2, pltpu.roll(scan, 2 * SLOT, 1), 1.0)
        ahead = jnp.where(slot_of >= 1, pltpu.roll(scan, SLOT, 1), 1.0)
        four = passed * pltpu.roll(passed, SLOT, 1)
        four = four * pltpu.roll(four, 2 * SLOT, 1)
        partner = jnp.where(odd_row, pltpu.roll(four, 1, 0), pltpu.roll(four, ROWS - 1, 0))
        ahead = ahead * jnp.where(odd_row, partner, 1.0)
        eight = four * partner
        other = pltpu.roll(eight, 4, 0)
        ahead = ahead * jnp.where(low, 1.0, other)
        if through is not None:
            ahead = ahead * through
        weight = ahead * (1.0 - passed)
        terms = (weight * mixed, weight * bend, weight * (mixed * mixed - 1.0))
        sums = terms if sums is None else tuple(x + y for x, y in zip(sums, terms))
        through = eight * other if through is None else through * (eight * other)
    rows_of = []
    for x in sums:
        x = x + pltpu.roll(x, SLOT, 1)
        x = x + pltpu.roll(x, 2 * SLOT, 1)
        x = x + pltpu.roll(x, 4, 0)
        rows_of.append(bright * (x + pltpu.roll(x, ROWS - 1, 0)))
    rows_of.append(1.0 - through)
    for c in range(4):
        out_ref[c, pl.ds(0, 1), :] = rows_of[c][:1, :own]
        out_ref[c, pl.ds(width - 1, 1), :] = rows_of[c][2:3, :own]

    z_copy.wait_send()
    outer_copies.wait_send()
    inner_copies.wait_send()
    for side, absent in ((0, left), (1, right)):

        @pl.when(jnp.logical_not(absent))
        def _():
            all_edges(side).wait_send()


def solution(mesh):
    n, tiles = mesh.shape["depth"], mesh.shape["tile"]

    def body(concentration, velocity, diffusivity):
        layers, width, rays = concentration.shape
        groups = width // ROWS
        own = rays // n
        assert own <= SLOT and LANES % own == 0 and layers == ROWS and groups == 4 and n % 2 == 0

        def block(*shape):
            return pltpu.VMEM(shape, jnp.float32)

        scratch = [
            block(layers, width + 2 * ROWS, rays),
            block(*velocity.shape),
            block(*diffusivity.shape),
            block(8, width, rays),
            block(4, ROWS, rays),
            block(4, ROWS, rays),
            block(n, ROWS, LANES),
            block(n, ROWS, LANES),
            block(n, ROWS, LANES),
            block(n, ROWS, LANES),
            block(n, 6, ROWS, LANES),
            block(n, ROWS, LANES),
            block(n, 3, ROWS, LANES),
            block(n, 3, ROWS, LANES),
            block(n, 5, ROWS, LANES),
            block(n, 5, ROWS, LANES),
            pltpu.SemaphoreType.REGULAR((2,)),
            pltpu.SemaphoreType.DMA((3,)),
            pltpu.SemaphoreType.DMA((2,)),
            pltpu.SemaphoreType.DMA((2,)),
            pltpu.SemaphoreType.DMA((2,)),
            pltpu.SemaphoreType.DMA((2,)),
            pltpu.SemaphoreType.DMA((2,)),
        ]
        return pl.pallas_call(
            functools.partial(kernel, n, tiles),
            out_shape=jax.ShapeDtypeStruct((4, width, own), jnp.float32),
            in_specs=[pl.BlockSpec(memory_space=pl.ANY)] * 3,
            out_specs=pl.BlockSpec(memory_space=pltpu.VMEM),
            scratch_shapes=scratch,
            compiler_params=pltpu.CompilerParams(collective_id=0, has_side_effects=True, vmem_limit_bytes=16 << 20),
        )(*[pltpu.with_memory_space_constraint(v, pltpu.HBM) for v in (concentration, velocity, diffusivity)])

    return jax.shard_map(
        body,
        mesh=mesh,
        in_specs=(
            P("depth", "tile", None),
            P(None, "depth", "tile", None),
            P("depth", "tile", None),
        ),
        out_specs=P(None, "tile", "depth"),
        check_vma=False,
    )
```

```python
import functools
import math

import jax
import jax.numpy as jnp
from jax import lax
from jax.experimental import pallas as pl
from jax.experimental.pallas import tpu as pltpu
from jax.sharding import PartitionSpec as P

ADVECT = 0.25
LANES = 128
ROWS = 8
SLOT = LANES // 4
MESH = pl.DeviceIdType.MESH
OUTER, INNER = 3, 5
EARLY = 2


def transpose_slots(tiles):
    slot = lax.broadcasted_iota(jnp.int32, (ROWS, LANES), 1) // SLOT
    a, b, c, d = tiles
    odd, high = slot % 2 == 1, slot >= 2

    def swap(x, y, step, mask):
        return (
            jnp.where(mask, pltpu.roll(y, step, 1), x),
            jnp.where(mask, y, pltpu.roll(x, LANES - step, 1)),
        )

    a, b = swap(a, b, SLOT, odd)
    c, d = swap(c, d, SLOT, odd)
    a, c = swap(a, c, 2 * SLOT, high)
    b, d = swap(b, d, 2 * SLOT, high)
    return a, b, c, d


def kernel(
    n,
    tiles,
    conc_hbm,
    vel_hbm,
    diff_hbm,
    out_ref,
    conc,
    vel,
    diff,
    values,
    edges,
    x_rows,
    x_send,
    x_recv,
    z_send,
    z_recv,
    held,
    held_edge,
    send,
    recv,
    ready,
    load_sem,
    z_sem,
    x_send_sem,
    x_recv_sem,
    outer_sem,
    inner_sem,
):
    layers, width, rays = diff.shape
    groups = width // ROWS
    own = rays // n
    per_tile = LANES // own
    total = layers * n
    half = 0.5 * ADVECT
    bright = math.sqrt(total)
    me = lax.axis_index("depth")
    lane_block = lax.axis_index("tile")
    left, right = lane_block == 0, lane_block == tiles - 1
    before_tile = lax.rem(lane_block + tiles - 1, tiles)
    after_tile = lax.rem(lane_block + 1, tiles)
    parity = lax.rem(me, 2)
    odd = parity == 1
    sibling = me + 1 - 2 * parity
    z_outer = parity * (layers - 1)
    z_inner = (1 - parity) * (layers - 1)

    barrier = pltpu.get_barrier_semaphore()
    load_conc = pltpu.make_async_copy(
        conc_hbm, conc.at[:, pl.ds(ROWS, width), :], load_sem.at[0]
    )
    load_conc.start()

    for k in range(1, n):
        pl.semaphore_signal(
            barrier, inc=1, device_id={"depth": lax.rem(me + k, n)}, device_id_type=MESH
        )

    @pl.when(jnp.logical_not(right))
    def _():
        for k in range(n):
            pl.semaphore_signal(barrier, inc=1, device_id=(k, after_tile), device_id_type=MESH)

    rest = pl.ds(1 - parity, layers - 1)
    first_loads = [
        pltpu.make_async_copy(vel_hbm.at[:, z_outer], vel.at[:, z_outer], load_sem.at[1]),
        pltpu.make_async_copy(diff_hbm.at[z_outer], diff.at[z_outer], load_sem.at[2]),
    ]
    last_loads = [
        pltpu.make_async_copy(vel_hbm.at[:, rest], vel.at[:, rest], load_sem.at[3]),
        pltpu.make_async_copy(diff_hbm.at[rest], diff.at[rest], load_sem.at[4]),
    ]
    for load in first_loads + last_loads:
        load.start()

    zero_rows = jnp.zeros((ROWS, rays), jnp.float32)
    for z in range(layers):
        conc[z, pl.ds(0, ROWS), :] = zero_rows
        conc[z, pl.ds(ROWS + width, ROWS), :] = zero_rows
    x_rows[...] = jnp.zeros_like(x_rows)

    @pl.when(left)
    def _():
        for k in range(n):
            x_recv[k, pl.ds(0, 2), :] = jnp.zeros((2, LANES), jnp.float32)

    @pl.when(right)
    def _():
        for k in range(n):
            x_recv[k, pl.ds(2, 2), :] = jnp.zeros((2, LANES), jnp.float32)

    slot_of = lax.broadcasted_iota(jnp.int32, (ROWS, LANES), 1) // SLOT
    sub = lax.broadcasted_iota(jnp.int32, (ROWS, LANES), 0)

    def pack(piece, store):
        for tile in range(rays // LANES):
            source = [piece(g, pl.ds(tile * LANES, LANES)) for g in range(4)]
            if own == SLOT:
                for j, block in enumerate(transpose_slots(source)):
                    store(tile * per_tile + j, block)
                continue
            for j in range(per_tile):
                block = None
                for g in range(4):
                    shift = (SLOT * g - j * own) % LANES
                    moved = pltpu.roll(source[g], shift, 1) if shift else source[g]
                    block = moved if block is None else jnp.where(slot_of == g, moved, block)
                store(tile * per_tile + j, block)

    def into(ref, *where):
        def store(k, block):
            ref[(k, *where)] = block

        return store

    load_conc.wait()
    for z in range(layers):
        q, r = z % 4, z // 4
        x_rows[q, pl.ds(r, 1), :] = conc[z, pl.ds(ROWS, 1), :]
        x_rows[q, pl.ds(2 + r, 1), :] = conc[z, pl.ds(ROWS + width - 1, 1), :]
    pack(lambda g, lanes: x_rows[g, :, lanes], into(x_send))
    pack(lambda g, lanes: conc[z_inner, pl.ds(ROWS + g * ROWS, ROWS), lanes], into(z_send))

    z_copy = pltpu.make_async_remote_copy(
        src_ref=z_send,
        dst_ref=z_recv,
        send_sem=z_sem.at[0],
        recv_sem=z_sem.at[1],
        device_id={"depth": sibling},
        device_id_type=MESH,
    )
    pl.semaphore_wait(barrier, n - 1 + n * jnp.where(left, 0, 1))
    z_copy.start()

    @pl.when(jnp.logical_not(left))
    def _():
        pl.semaphore_signal(ready.at[1], inc=1, device_id=(me, before_tile), device_id_type=MESH)

    def to_left(k):
        return pltpu.make_async_remote_copy(
            src_ref=x_send.at[k, pl.ds(0, 2)],
            dst_ref=x_recv.at[me, pl.ds(2, 2)],
            send_sem=x_send_sem.at[0],
            recv_sem=x_recv_sem.at[1],
            device_id=(k, before_tile),
            device_id_type=MESH,
        )

    def to_right(k):
        return pltpu.make_async_remote_copy(
            src_ref=x_send.at[k, pl.ds(2, 2)],
            dst_ref=x_recv.at[me, pl.ds(0, 2)],
            send_sem=x_send_sem.at[1],
            recv_sem=x_recv_sem.at[0],
            device_id=(k, after_tile),
            device_id_type=MESH,
        )

    @pl.when(jnp.logical_not(left))
    def _():
        for k in range(n):
            to_left(k).start()

    pack(lambda g, lanes: conc[z_outer, pl.ds(ROWS + g * ROWS, ROWS), lanes], into(send, 2))
    for load in first_loads:
        load.wait()

    lane = lax.broadcasted_iota(jnp.int32, (ROWS, rays), 1)

    def local_update(z, start, sign=None):
        rows = pl.ds(start, ROWS)
        here = conc[z, pl.ds(ROWS + start, ROWS), :]
        left_cells = conc[z, pl.ds(ROWS + start - 1, ROWS), :]
        right_cells = conc[z, pl.ds(ROWS + start + 1, ROWS), :]
        lower_cells = jnp.where(lane == 0, 0.0, pltpu.roll(here, 1, 1))
        upper_cells = jnp.where(lane == rays - 1, 0.0, pltpu.roll(here, rays - 1, 1))
        spread = left_cells + right_cells + lower_cells + upper_cells
        flow = vel[1, z, rows, :] * (right_cells - left_cells) + vel[2, z, rows, :] * (
            upper_cells - lower_cells
        )
        if sign is None:
            back = conc[z - 1, pl.ds(ROWS + start, ROWS), :]
            front = conc[z + 1, pl.ds(ROWS + start, ROWS), :]
            spread = spread + (back + front)
            slope = front - back
        else:
            step, factor = sign
            beside = conc[z + step, pl.ds(ROWS + start, ROWS), :]
            spread = spread + beside
            slope = factor * beside
        flow = flow + vel[0, z, rows, :] * slope
        return here + diff[z, rows, :] * (spread - 6.0 * here) - half * flow

    def shade(mixed):
        bend = jnp.tanh(mixed)
        passed = jnp.exp((bend + 2.0) * (-1.0 / total))
        return bend, passed

    def add_cell(state, mixed):
        bend, passed = shade(mixed)
        if state is None:
            weight = 1.0 - passed
            return weight * mixed, weight * bend, weight * (mixed * mixed - 1.0), passed
        one, two, three, through = state
        weight = through * (1.0 - passed)
        return (
            one + weight * mixed,
            two + weight * bend,
            three + weight * (mixed * mixed - 1.0),
            through * passed,
        )

    toward = jnp.where(odd, -1.0, 1.0)

    def boundary(z, step, factor, v):
        for g in range(groups):
            rows = pl.ds(g * ROWS, ROWS)
            values[v, rows, :] = local_update(z, g * ROWS, (step, factor))
            values[v + 1, rows, :] = diff[z, rows, :] + (half * factor) * vel[0, z, rows, :]

    boundary(z_outer, 1 - 2 * parity, toward, 0)

    def piece_of(v):
        return lambda g, lanes: values[v, pl.ds(g * ROWS, ROWS), lanes]

    for i in range(2):
        pack(piece_of(i), into(send, i))

    def part(target, k, slots, sems):
        return pltpu.make_async_remote_copy(
            src_ref=send.at[target, slots],
            dst_ref=recv.at[k, slots],
            send_sem=sems.at[0],
            recv_sem=sems.at[1],
            device_id={"depth": target},
            device_id_type=MESH,
        )

    soon = me < EARLY
    outer, inner = pl.ds(0, OUTER), pl.ds(OUTER, INNER)
    both = pl.ds(0, OUTER + INNER)

    def to_early(slots, sems):
        for d in range(EARLY):

            @pl.when(me != d)
            def _():
                part(d, lax.rem(d + n - me, n), slots, sems).start()

    to_early(outer, outer_sem)

    for load in last_loads:
        load.wait()

    boundary(z_inner, 2 * parity - 1, -toward, 2)

    first_row, last_row = pl.ds(0, 1), pl.ds(width - 1, 1)

    def note_gain(z):
        q, r = z % 4, z // 4
        edges[q, pl.ds(4 + r, 1), :] = diff[z, first_row, :] + half * vel[1, z, first_row, :]
        edges[q, pl.ds(6 + r, 1), :] = diff[z, last_row, :] - half * vel[1, z, last_row, :]

    for g in range(groups):
        state = None
        for z in range(1, layers - 1):
            mixed = local_update(z, g * ROWS)
            if g == 0:
                edges[z % 4, pl.ds(z // 4, 1), :] = mixed[:1]
            if g == groups - 1:
                edges[z % 4, pl.ds(2 + z // 4, 1), :] = mixed[ROWS - 1 :]
            state = add_cell(state, mixed)
        for c in range(4):
            values[4 + c, pl.ds(g * ROWS, ROWS), :] = state[c]
    for z in range(layers):
        note_gain(z)
    for e, row in enumerate((first_row, last_row)):
        ends = values[0, row, :], values[2, row, :]
        edges[0, pl.ds(2 * e, 1), :] = jnp.where(odd, ends[1], ends[0])
        edges[3, pl.ds(2 * e + 1, 1), :] = jnp.where(odd, ends[0], ends[1])
    for v in range(6):
        pack(piece_of(2 + v), into(held, v))
    pack(lambda g, lanes: edges[g, :, lanes], into(held_edge))

    def into_edges(change, z):
        if z == 0:
            first, last = change, pltpu.roll(pltpu.roll(change, SLOT, 1), 3, 0)
            where = slot_of == 0, sub == 0, sub == 2
        else:
            first = pltpu.roll(pltpu.roll(change, LANES - SLOT, 1), 1, 0)
            last = pltpu.roll(change, 4, 0)
            where = slot_of == 3, sub == 1, sub == 3
        moved = jnp.where(where[1], first, jnp.where(where[2], last, 0.0))
        return jnp.where(where[0], moved, 0.0)

    z_copy.wait_recv()
    def finish(k):
        change = held[k, 1] * z_recv[k]
        mixed = held[k, 0] + change
        bend, passed = shade(mixed)
        through = held[k, 5]
        weight = 1.0 - passed
        scale = jnp.where(odd, passed, 1.0)
        weight = jnp.where(odd, weight, weight * through)
        for c, term in enumerate((mixed, bend, mixed * mixed - 1.0)):
            send[k, OUTER + c] = scale * held[k, 2 + c] + weight * term
        send[k, OUTER + 3] = through * passed
        send[k, OUTER + 4] = held_edge[k] + jnp.where(
            odd, into_edges(change, 0), into_edges(change, layers - 1)
        )

    def all_of(first, count, slots, sems):
        return pltpu.make_async_remote_copy(
            src_ref=send.at[pl.ds(first, count), slots],
            dst_ref=recv.at[pl.ds(first, count), slots],
            send_sem=sems.at[0],
            recv_sem=sems.at[1],
            device_id={"depth": sibling},
            device_id_type=MESH,
        )

    for k in range(EARLY):
        finish(k)
    to_early(inner, inner_sem)
    for k in range(EARLY, n):
        finish(k)
    for k in range(1, n):
        target = lax.rem(me + k, n)

        @pl.when(target >= EARLY)
        def _():
            part(target, k, both, inner_sem).start()

    @pl.when(jnp.logical_not(right))
    def _():
        pl.semaphore_wait(ready.at[1], 1)
        for k in range(n):
            to_right(k).start()

    recv[0] = send[me]

    def all_edges(side):
        return pltpu.make_async_remote_copy(
            src_ref=x_send.at[:, pl.ds(2 * side, 2)],
            dst_ref=x_recv.at[:, pl.ds(2 * side, 2)],
            send_sem=x_send_sem.at[side],
            recv_sem=x_recv_sem.at[side],
            device_id={"depth": sibling},
            device_id_type=MESH,
        )

    @pl.when(soon)
    def _():
        all_of(1, n - 1, outer, outer_sem).wait_recv()

    @pl.when(jnp.logical_not(soon))
    def _():
        all_of(1, n - 1, both, inner_sem).wait_recv()

    index = [lax.rem(me - s + n, n) for s in range(n)]
    cells = []
    edge_cells = []
    for s in range(n):
        beyond = s - 1 if s % 2 == 0 else s + 1
        mixed = recv[index[s], 0]
        change = None
        if 0 <= beyond < n:
            change = recv[index[s], 1] * recv[index[beyond], 2]
            mixed = mixed + change
            change = into_edges(change, 0 if s % 2 == 0 else layers - 1)
        bend, passed = shade(mixed)
        cells.append((mixed, bend, mixed * mixed - 1.0, passed))
        edge_cells.append(change)

    @pl.when(soon)
    def _():
        all_of(1, n - 1, inner, inner_sem).wait_recv()

    state = None
    for s in range(n):
        bricks = [None, None]
        *terms, passed = cells[s]
        weight = 1.0 - passed
        bricks[s % 2] = tuple(weight * x for x in terms) + (passed,)
        bricks[1 - s % 2] = tuple(recv[index[s], OUTER + c] for c in range(4))
        for brick in bricks:
            if state is None:
                state = brick
            else:
                through = state[3]
                state = tuple(state[c] + through * brick[c] for c in range(3)) + (
                    through * brick[3],
                )
    picture = [bright * state[c] for c in range(3)] + [1.0 - state[3]]
    for c in range(4):
        for g in range(groups):
            color = pltpu.roll(picture[c], LANES - SLOT * g, 1) if g else picture[c]
            out_ref[c, pl.ds(g * ROWS, ROWS), :] = color[:, :own]

    for side, absent in ((0, left), (1, right)):

        @pl.when(jnp.logical_not(absent))
        def _():
            all_edges(side).wait_recv()

    through = None
    sums = None
    odd_row, low = sub % 2 == 1, sub < 4
    for s in range(0, n, 2):
        two = []
        for i in (s, s + 1):
            packed = recv[index[i], OUTER + 4]
            mixed = packed + pltpu.roll(packed, 4, 0) * x_recv[i]
            two.append(mixed if edge_cells[i] is None else mixed + edge_cells[i])
        mixed = jnp.where(low, two[0], pltpu.roll(two[1], 4, 0))
        bend, passed = shade(mixed)
        scan = passed * jnp.where(slot_of >= 1, pltpu.roll(passed, SLOT, 1), 1.0)
        scan = scan * jnp.where(slot_of >= 2, pltpu.roll(scan, 2 * SLOT, 1), 1.0)
        ahead = jnp.where(slot_of >= 1, pltpu.roll(scan, SLOT, 1), 1.0)
        four = passed * pltpu.roll(passed, SLOT, 1)
        four = four * pltpu.roll(four, 2 * SLOT, 1)
        partner = jnp.where(odd_row, pltpu.roll(four, 1, 0), pltpu.roll(four, ROWS - 1, 0))
        ahead = ahead * jnp.where(odd_row, partner, 1.0)
        eight = four * partner
        other = pltpu.roll(eight, 4, 0)
        ahead = ahead * jnp.where(low, 1.0, other)
        if through is not None:
            ahead = ahead * through
        weight = ahead * (1.0 - passed)
        terms = (weight * mixed, weight * bend, weight * (mixed * mixed - 1.0))
        sums = terms if sums is None else tuple(x + y for x, y in zip(sums, terms))
        through = eight * other if through is None else through * (eight * other)
    rows_of = []
    for x in sums:
        x = x + pltpu.roll(x, SLOT, 1)
        x = x + pltpu.roll(x, 2 * SLOT, 1)
        x = x + pltpu.roll(x, 4, 0)
        rows_of.append(bright * (x + pltpu.roll(x, ROWS - 1, 0)))
    rows_of.append(1.0 - through)
    for c in range(4):
        out_ref[c, pl.ds(0, 1), :] = rows_of[c][:1, :own]
        out_ref[c, pl.ds(width - 1, 1), :] = rows_of[c][2:3, :own]

    z_copy.wait_send()

    @pl.when(soon)
    def _():
        all_of(0, EARLY - 1, outer, outer_sem).wait_send()
        all_of(0, EARLY - 1, inner, inner_sem).wait_send()

    @pl.when(jnp.logical_not(soon))
    def _():
        all_of(0, EARLY, outer, outer_sem).wait_send()
        all_of(0, EARLY, inner, inner_sem).wait_send()

    @pl.when(soon)
    def _():
        all_of(0, n - EARLY, both, inner_sem).wait_send()

    @pl.when(jnp.logical_not(soon))
    def _():
        all_of(0, n - EARLY - 1, both, inner_sem).wait_send()
    for side, absent in ((0, left), (1, right)):

        @pl.when(jnp.logical_not(absent))
        def _():
            all_edges(side).wait_send()


def solution(mesh):
    n, tiles = mesh.shape["depth"], mesh.shape["tile"]

    def body(concentration, velocity, diffusivity):
        layers, width, rays = concentration.shape
        groups = width // ROWS
        own = rays // n
        assert own <= SLOT and LANES % own == 0 and layers == ROWS and groups == 4 and n % 2 == 0

        def block(*shape):
            return pltpu.VMEM(shape, jnp.float32)

        scratch = [
            block(layers, width + 2 * ROWS, rays),
            block(*velocity.shape),
            block(*diffusivity.shape),
            block(8, width, rays),
            block(4, ROWS, rays),
            block(4, ROWS, rays),
            block(n, ROWS, LANES),
            block(n, ROWS, LANES),
            block(n, ROWS, LANES),
            block(n, ROWS, LANES),
            block(n, 6, ROWS, LANES),
            block(n, ROWS, LANES),
            block(n, OUTER + INNER, ROWS, LANES),
            block(n, OUTER + INNER, ROWS, LANES),
            pltpu.SemaphoreType.REGULAR((2,)),
            pltpu.SemaphoreType.DMA((5,)),
            pltpu.SemaphoreType.DMA((2,)),
            pltpu.SemaphoreType.DMA((2,)),
            pltpu.SemaphoreType.DMA((2,)),
            pltpu.SemaphoreType.DMA((2,)),
            pltpu.SemaphoreType.DMA((2,)),
        ]
        return pl.pallas_call(
            functools.partial(kernel, n, tiles),
            out_shape=jax.ShapeDtypeStruct((4, width, own), jnp.float32),
            in_specs=[pl.BlockSpec(memory_space=pl.ANY)] * 3,
            out_specs=pl.BlockSpec(memory_space=pltpu.VMEM),
            scratch_shapes=scratch,
            compiler_params=pltpu.CompilerParams(collective_id=0, has_side_effects=True, vmem_limit_bytes=16 << 20),
        )(*[pltpu.with_memory_space_constraint(v, pltpu.HBM) for v in (concentration, velocity, diffusivity)])

    return jax.shard_map(
        body,
        mesh=mesh,
        in_specs=(
            P("depth", "tile", None),
            P(None, "depth", "tile", None),
            P("depth", "tile", None),
        ),
        out_specs=P(None, "tile", "depth"),
        check_vma=False,
    )
```

```python
import functools
import math

import jax
import jax.numpy as jnp
from jax import lax
from jax.experimental import pallas as pl
from jax.experimental.pallas import tpu as pltpu
from jax.sharding import PartitionSpec as P

ADVECT = 0.25
LANES = 128
ROWS = 8
SLOT = LANES // 4
MESH = pl.DeviceIdType.MESH
OUTER, INNER = 3, 5
EARLY = 2


def transpose_slots(tiles):
    slot = lax.broadcasted_iota(jnp.int32, (ROWS, LANES), 1) // SLOT
    a, b, c, d = tiles
    odd, high = slot % 2 == 1, slot >= 2

    def swap(x, y, step, mask):
        return (
            jnp.where(mask, pltpu.roll(y, step, 1), x),
            jnp.where(mask, y, pltpu.roll(x, LANES - step, 1)),
        )

    a, b = swap(a, b, SLOT, odd)
    c, d = swap(c, d, SLOT, odd)
    a, c = swap(a, c, 2 * SLOT, high)
    b, d = swap(b, d, 2 * SLOT, high)
    return a, b, c, d


def kernel(
    n,
    tiles,
    conc_hbm,
    vel_hbm,
    diff_hbm,
    out_ref,
    conc,
    vel,
    diff,
    values,
    edges,
    x_rows,
    x_send,
    x_recv,
    z_send,
    z_recv,
    held,
    held_edge,
    send,
    recv,
    ready,
    load_sem,
    z_sem,
    x_send_sem,
    x_recv_sem,
    outer_sem,
    inner_sem,
):
    layers, width, rays = diff.shape
    groups = width // ROWS
    own = rays // n
    per_tile = LANES // own
    total = layers * n
    half = 0.5 * ADVECT
    bright = math.sqrt(total)
    me = lax.axis_index("depth")
    lane_block = lax.axis_index("tile")
    left, right = lane_block == 0, lane_block == tiles - 1
    before_tile = lax.rem(lane_block + tiles - 1, tiles)
    after_tile = lax.rem(lane_block + 1, tiles)
    parity = lax.rem(me, 2)
    odd = parity == 1
    sibling = me + 1 - 2 * parity
    z_outer = parity * (layers - 1)
    z_inner = (1 - parity) * (layers - 1)

    barrier = pltpu.get_barrier_semaphore()
    load_conc = pltpu.make_async_copy(
        conc_hbm, conc.at[:, pl.ds(ROWS, width), :], load_sem.at[0]
    )
    load_conc.start()

    for k in range(1, n):
        pl.semaphore_signal(
            barrier, inc=1, device_id={"depth": lax.rem(me + k, n)}, device_id_type=MESH
        )

    @pl.when(jnp.logical_not(right))
    def _():
        for k in range(n):
            pl.semaphore_signal(barrier, inc=1, device_id=(k, after_tile), device_id_type=MESH)

    rest = pl.ds(1 - parity, layers - 1)
    first_loads = [
        pltpu.make_async_copy(vel_hbm.at[:, z_outer], vel.at[:, z_outer], load_sem.at[1]),
        pltpu.make_async_copy(diff_hbm.at[z_outer], diff.at[z_outer], load_sem.at[2]),
    ]
    last_loads = [
        pltpu.make_async_copy(vel_hbm.at[:, rest], vel.at[:, rest], load_sem.at[3]),
        pltpu.make_async_copy(diff_hbm.at[rest], diff.at[rest], load_sem.at[4]),
    ]
    for load in first_loads + last_loads:
        load.start()

    zero_rows = jnp.zeros((ROWS, rays), jnp.float32)
    for z in range(layers):
        conc[z, pl.ds(0, ROWS), :] = zero_rows
        conc[z, pl.ds(ROWS + width, ROWS), :] = zero_rows
    x_rows[...] = jnp.zeros_like(x_rows)

    @pl.when(left)
    def _():
        for k in range(n):
            x_recv[k, pl.ds(0, 2), :] = jnp.zeros((2, LANES), jnp.float32)

    @pl.when(right)
    def _():
        for k in range(n):
            x_recv[k, pl.ds(2, 2), :] = jnp.zeros((2, LANES), jnp.float32)

    slot_of = lax.broadcasted_iota(jnp.int32, (ROWS, LANES), 1) // SLOT
    sub = lax.broadcasted_iota(jnp.int32, (ROWS, LANES), 0)

    def pack(piece, store):
        for tile in range(rays // LANES):
            source = [piece(g, pl.ds(tile * LANES, LANES)) for g in range(4)]
            if own == SLOT:
                for j, block in enumerate(transpose_slots(source)):
                    store(tile * per_tile + j, block)
                continue
            for j in range(per_tile):
                block = None
                for g in range(4):
                    shift = (SLOT * g - j * own) % LANES
                    moved = pltpu.roll(source[g], shift, 1) if shift else source[g]
                    block = moved if block is None else jnp.where(slot_of == g, moved, block)
                store(tile * per_tile + j, block)

    def into(ref, *where):
        def store(k, block):
            ref[(k, *where)] = block

        return store

    load_conc.wait()
    for z in range(layers):
        q, r = z % 4, z // 4
        x_rows[q, pl.ds(r, 1), :] = conc[z, pl.ds(ROWS, 1), :]
        x_rows[q, pl.ds(2 + r, 1), :] = conc[z, pl.ds(ROWS + width - 1, 1), :]
    pack(lambda g, lanes: x_rows[g, :, lanes], into(x_send))
    pack(lambda g, lanes: conc[z_inner, pl.ds(ROWS + g * ROWS, ROWS), lanes], into(z_send))

    z_copy = pltpu.make_async_remote_copy(
        src_ref=z_send,
        dst_ref=z_recv,
        send_sem=z_sem.at[0],
        recv_sem=z_sem.at[1],
        device_id={"depth": sibling},
        device_id_type=MESH,
    )
    def to_left(k):
        return pltpu.make_async_remote_copy(
            src_ref=x_send.at[k, pl.ds(0, 2)],
            dst_ref=x_recv.at[me, pl.ds(2, 2)],
            send_sem=x_send_sem.at[0],
            recv_sem=x_recv_sem.at[1],
            device_id=(k, before_tile),
            device_id_type=MESH,
        )

    def to_right(k):
        return pltpu.make_async_remote_copy(
            src_ref=x_send.at[k, pl.ds(2, 2)],
            dst_ref=x_recv.at[me, pl.ds(0, 2)],
            send_sem=x_send_sem.at[1],
            recv_sem=x_recv_sem.at[0],
            device_id=(k, after_tile),
            device_id_type=MESH,
        )

    pack(lambda g, lanes: conc[z_outer, pl.ds(ROWS + g * ROWS, ROWS), lanes], into(send, 2))
    for load in first_loads:
        load.wait()

    lane = lax.broadcasted_iota(jnp.int32, (ROWS, rays), 1)

    def local_update(z, start, sign=None):
        rows = pl.ds(start, ROWS)
        here = conc[z, pl.ds(ROWS + start, ROWS), :]
        left_cells = conc[z, pl.ds(ROWS + start - 1, ROWS), :]
        right_cells = conc[z, pl.ds(ROWS + start + 1, ROWS), :]
        lower_cells = jnp.where(lane == 0, 0.0, pltpu.roll(here, 1, 1))
        upper_cells = jnp.where(lane == rays - 1, 0.0, pltpu.roll(here, rays - 1, 1))
        spread = left_cells + right_cells + lower_cells + upper_cells
        flow = vel[1, z, rows, :] * (right_cells - left_cells) + vel[2, z, rows, :] * (
            upper_cells - lower_cells
        )
        if sign is None:
            back = conc[z - 1, pl.ds(ROWS + start, ROWS), :]
            front = conc[z + 1, pl.ds(ROWS + start, ROWS), :]
            spread = spread + (back + front)
            slope = front - back
        else:
            step, factor = sign
            beside = conc[z + step, pl.ds(ROWS + start, ROWS), :]
            spread = spread + beside
            slope = factor * beside
        flow = flow + vel[0, z, rows, :] * slope
        return here + diff[z, rows, :] * (spread - 6.0 * here) - half * flow

    def shade(mixed):
        bend = jnp.tanh(mixed)
        passed = jnp.exp((bend + 2.0) * (-1.0 / total))
        return bend, passed

    def add_cell(state, mixed):
        bend, passed = shade(mixed)
        if state is None:
            weight = 1.0 - passed
            return weight * mixed, weight * bend, weight * (mixed * mixed - 1.0), passed
        one, two, three, through = state
        weight = through * (1.0 - passed)
        return (
            one + weight * mixed,
            two + weight * bend,
            three + weight * (mixed * mixed - 1.0),
            through * passed,
        )

    toward = jnp.where(odd, -1.0, 1.0)

    def boundary(z, step, factor, v):
        for g in range(groups):
            rows = pl.ds(g * ROWS, ROWS)
            values[v, rows, :] = local_update(z, g * ROWS, (step, factor))
            values[v + 1, rows, :] = diff[z, rows, :] + (half * factor) * vel[0, z, rows, :]

    boundary(z_outer, 1 - 2 * parity, toward, 0)

    def piece_of(v):
        return lambda g, lanes: values[v, pl.ds(g * ROWS, ROWS), lanes]

    for i in range(2):
        pack(piece_of(i), into(send, i))

    def part(target, k, slots, sems):
        return pltpu.make_async_remote_copy(
            src_ref=send.at[target, slots],
            dst_ref=recv.at[k, slots],
            send_sem=sems.at[0],
            recv_sem=sems.at[1],
            device_id={"depth": target},
            device_id_type=MESH,
        )

    outer, inner = pl.ds(0, OUTER), pl.ds(OUTER, INNER)

    def part_to(d, slots, sems):
        @pl.when(me != d)
        def _():
            part(d, lax.rem(d + n - me, n), slots, sems).start()

    def parts_beyond(slots, sems):
        for k in range(1, n):
            target = lax.rem(me + k, n)

            @pl.when(target >= EARLY)
            def _():
                part(target, k, slots, sems).start()

    pl.semaphore_wait(barrier, n - 1 + n * jnp.where(left, 0, 1))
    z_copy.start()
    for d in range(EARLY):
        part_to(d, outer, outer_sem)
    parts_beyond(outer, outer_sem)

    @pl.when(jnp.logical_not(left))
    def _():
        pl.semaphore_signal(ready.at[1], inc=1, device_id=(me, before_tile), device_id_type=MESH)

    @pl.when(jnp.logical_not(left))
    def _():
        for k in range(n):
            to_left(k).start()

    for load in last_loads:
        load.wait()

    boundary(z_inner, 2 * parity - 1, -toward, 2)

    first_row, last_row = pl.ds(0, 1), pl.ds(width - 1, 1)

    def note_gain(z):
        q, r = z % 4, z // 4
        edges[q, pl.ds(4 + r, 1), :] = diff[z, first_row, :] + half * vel[1, z, first_row, :]
        edges[q, pl.ds(6 + r, 1), :] = diff[z, last_row, :] - half * vel[1, z, last_row, :]

    for g in range(groups):
        state = None
        for z in range(1, layers - 1):
            mixed = local_update(z, g * ROWS)
            if g == 0:
                edges[z % 4, pl.ds(z // 4, 1), :] = mixed[:1]
            if g == groups - 1:
                edges[z % 4, pl.ds(2 + z // 4, 1), :] = mixed[ROWS - 1 :]
            state = add_cell(state, mixed)
        for c in range(4):
            values[4 + c, pl.ds(g * ROWS, ROWS), :] = state[c]
    for z in range(layers):
        note_gain(z)
    for e, row in enumerate((first_row, last_row)):
        ends = values[0, row, :], values[2, row, :]
        edges[0, pl.ds(2 * e, 1), :] = jnp.where(odd, ends[1], ends[0])
        edges[3, pl.ds(2 * e + 1, 1), :] = jnp.where(odd, ends[0], ends[1])
    for v in range(6):
        pack(piece_of(2 + v), into(held, v))
    pack(lambda g, lanes: edges[g, :, lanes], into(held_edge))

    def into_edges(change, z):
        if z == 0:
            first, last = change, pltpu.roll(pltpu.roll(change, SLOT, 1), 3, 0)
            where = slot_of == 0, sub == 0, sub == 2
        else:
            first = pltpu.roll(pltpu.roll(change, LANES - SLOT, 1), 1, 0)
            last = pltpu.roll(change, 4, 0)
            where = slot_of == 3, sub == 1, sub == 3
        moved = jnp.where(where[1], first, jnp.where(where[2], last, 0.0))
        return jnp.where(where[0], moved, 0.0)

    z_copy.wait_recv()
    def finish(k):
        change = held[k, 1] * z_recv[k]
        mixed = held[k, 0] + change
        bend, passed = shade(mixed)
        through = held[k, 5]
        weight = 1.0 - passed
        scale = jnp.where(odd, passed, 1.0)
        weight = jnp.where(odd, weight, weight * through)
        for c, term in enumerate((mixed, bend, mixed * mixed - 1.0)):
            send[k, OUTER + c] = scale * held[k, 2 + c] + weight * term
        send[k, OUTER + 3] = through * passed
        packed = held_edge[k] + jnp.where(
            odd, into_edges(change, 0), into_edges(change, layers - 1)
        )
        send[k, OUTER + 4] = jnp.where(odd, pltpu.roll(packed, 4, 0), packed)

    def all_of(slots, sems):
        others = pl.ds(1, n - 1)
        return pltpu.make_async_remote_copy(
            src_ref=send.at[others, slots],
            dst_ref=recv.at[others, slots],
            send_sem=sems.at[0],
            recv_sem=sems.at[1],
            device_id={"depth": sibling},
            device_id_type=MESH,
        )

    for d in range(EARLY):
        finish(d)
    for d in range(EARLY):
        part_to(d, inner, inner_sem)
    for k in range(EARLY, n):
        finish(k)
    parts_beyond(inner, inner_sem)

    @pl.when(jnp.logical_not(right))
    def _():
        pl.semaphore_wait(ready.at[1], 1)
        for k in range(n):
            to_right(k).start()

    recv[0] = send[me]

    def all_edges(side):
        return pltpu.make_async_remote_copy(
            src_ref=x_send.at[:, pl.ds(2 * side, 2)],
            dst_ref=x_recv.at[:, pl.ds(2 * side, 2)],
            send_sem=x_send_sem.at[side],
            recv_sem=x_recv_sem.at[side],
            device_id={"depth": sibling},
            device_id_type=MESH,
        )

    outer_copies, inner_copies = all_of(outer, outer_sem), all_of(inner, inner_sem)
    outer_copies.wait_recv()
    index = [lax.rem(me - s + n, n) for s in range(n)]
    cells = []
    edge_cells = []
    for s in range(n):
        beyond = s - 1 if s % 2 == 0 else s + 1
        mixed = recv[index[s], 0]
        change = None
        if 0 <= beyond < n:
            change = recv[index[s], 1] * recv[index[beyond], 2]
            mixed = mixed + change
            change = into_edges(change, 0 if s % 2 == 0 else layers - 1)
        bend, passed = shade(mixed)
        cells.append((mixed, bend, mixed * mixed - 1.0, passed))
        edge_cells.append(pltpu.roll(change, 4, 0) if s % 2 == 1 and change is not None else change)

    for side, absent in ((0, left), (1, right)):

        @pl.when(jnp.logical_not(absent))
        def _():
            all_edges(side).wait_recv()

    beside_cells = [x_recv[i] if i % 2 == 0 else pltpu.roll(x_recv[i], 4, 0) for i in range(n)]

    inner_copies.wait_recv()
    state = None
    for s in range(n):
        bricks = [None, None]
        *terms, passed = cells[s]
        weight = 1.0 - passed
        bricks[s % 2] = tuple(weight * x for x in terms) + (passed,)
        bricks[1 - s % 2] = tuple(recv[index[s], OUTER + c] for c in range(4))
        for brick in bricks:
            if state is None:
                state = brick
            else:
                through = state[3]
                state = tuple(state[c] + through * brick[c] for c in range(3)) + (
                    through * brick[3],
                )
    picture = [bright * state[c] for c in range(3)] + [1.0 - state[3]]
    for c in range(4):
        for g in range(groups):
            color = pltpu.roll(picture[c], LANES - SLOT * g, 1) if g else picture[c]
            out_ref[c, pl.ds(g * ROWS, ROWS), :] = color[:, :own]

    through = None
    sums = None
    odd_row, low = sub % 2 == 1, sub < 4
    for s in range(0, n, 2):
        two = []
        for i in (s, s + 1):
            packed = recv[index[i], OUTER + 4]
            mixed = packed + pltpu.roll(packed, 4, 0) * beside_cells[i]
            two.append(mixed if edge_cells[i] is None else mixed + edge_cells[i])
        mixed = jnp.where(low, two[0], two[1])
        bend, passed = shade(mixed)
        ahead, four = None, passed
        for q in range(1, 4):
            moved = pltpu.roll(passed, q * SLOT, 1)
            four = four * moved
            moved = jnp.where(slot_of >= q, moved, 1.0)
            ahead = moved if ahead is None else ahead * moved
        by = {q: pltpu.roll(four, q, 0) for q in (1, 3, 4, 5, 7)}
        partner = jnp.where(odd_row, by[1], by[7])
        other = by[4] * jnp.where(odd_row, by[5], by[3])
        ahead = ahead * jnp.where(odd_row, partner, 1.0) * jnp.where(low, 1.0, other)
        eight = four * partner
        if through is not None:
            ahead = ahead * through
        weight = ahead * (1.0 - passed)
        terms = (weight * mixed, weight * bend, weight * (mixed * mixed - 1.0))
        sums = terms if sums is None else tuple(x + y for x, y in zip(sums, terms))
        through = eight * other if through is None else through * (eight * other)
    rows_of = []
    for x in sums:
        x = (x + pltpu.roll(x, SLOT, 1)) + (pltpu.roll(x, 2 * SLOT, 1) + pltpu.roll(x, 3 * SLOT, 1))
        x = (x + pltpu.roll(x, 4, 0)) + (pltpu.roll(x, 3, 0) + pltpu.roll(x, 7, 0))
        rows_of.append(bright * x)
    rows_of.append(1.0 - through)
    for c in range(4):
        out_ref[c, pl.ds(0, 1), :] = rows_of[c][:1, :own]
        out_ref[c, pl.ds(width - 1, 1), :] = rows_of[c][2:3, :own]

    z_copy.wait_send()

    outer_copies.wait_send()
    inner_copies.wait_send()
    for side, absent in ((0, left), (1, right)):

        @pl.when(jnp.logical_not(absent))
        def _():
            all_edges(side).wait_send()


def solution(mesh):
    n, tiles = mesh.shape["depth"], mesh.shape["tile"]

    def body(concentration, velocity, diffusivity):
        layers, width, rays = concentration.shape
        groups = width // ROWS
        own = rays // n
        assert own <= SLOT and LANES % own == 0 and layers == ROWS and groups == 4 and n % 2 == 0

        def block(*shape):
            return pltpu.VMEM(shape, jnp.float32)

        scratch = [
            block(layers, width + 2 * ROWS, rays),
            block(*velocity.shape),
            block(*diffusivity.shape),
            block(8, width, rays),
            block(4, ROWS, rays),
            block(4, ROWS, rays),
            block(n, ROWS, LANES),
            block(n, ROWS, LANES),
            block(n, ROWS, LANES),
            block(n, ROWS, LANES),
            block(n, 6, ROWS, LANES),
            block(n, ROWS, LANES),
            block(n, OUTER + INNER, ROWS, LANES),
            block(n, OUTER + INNER, ROWS, LANES),
            pltpu.SemaphoreType.REGULAR((2,)),
            pltpu.SemaphoreType.DMA((5,)),
            pltpu.SemaphoreType.DMA((2,)),
            pltpu.SemaphoreType.DMA((2,)),
            pltpu.SemaphoreType.DMA((2,)),
            pltpu.SemaphoreType.DMA((2,)),
            pltpu.SemaphoreType.DMA((2,)),
        ]
        return pl.pallas_call(
            functools.partial(kernel, n, tiles),
            out_shape=jax.ShapeDtypeStruct((4, width, own), jnp.float32),
            in_specs=[pl.BlockSpec(memory_space=pl.ANY)] * 3,
            out_specs=pl.BlockSpec(memory_space=pltpu.VMEM),
            scratch_shapes=scratch,
            compiler_params=pltpu.CompilerParams(collective_id=0, has_side_effects=True, vmem_limit_bytes=16 << 20),
        )(*[pltpu.with_memory_space_constraint(v, pltpu.HBM) for v in (concentration, velocity, diffusivity)])

    return jax.shard_map(
        body,
        mesh=mesh,
        in_specs=(
            P("depth", "tile", None),
            P(None, "depth", "tile", None),
            P("depth", "tile", None),
        ),
        out_specs=P(None, "tile", "depth"),
        check_vma=False,
    )
```

```python
import functools
import math

import jax
import jax.numpy as jnp
from jax import lax
from jax.experimental import pallas as pl
from jax.experimental.pallas import tpu as pltpu
from jax.sharding import PartitionSpec as P

ADVECT = 0.25
LANES = 128
ROWS = 8
SLOT = LANES // 4
MESH = pl.DeviceIdType.MESH
OUTER, INNER = 3, 5
EARLY = 2


def transpose_slots(tiles):
    slot = lax.broadcasted_iota(jnp.int32, (ROWS, LANES), 1) // SLOT
    a, b, c, d = tiles
    odd, high = slot % 2 == 1, slot >= 2

    def swap(x, y, step, mask):
        return (
            jnp.where(mask, pltpu.roll(y, step, 1), x),
            jnp.where(mask, y, pltpu.roll(x, LANES - step, 1)),
        )

    a, b = swap(a, b, SLOT, odd)
    c, d = swap(c, d, SLOT, odd)
    a, c = swap(a, c, 2 * SLOT, high)
    b, d = swap(b, d, 2 * SLOT, high)
    return a, b, c, d


def kernel(
    n,
    tiles,
    conc_hbm,
    vel_hbm,
    diff_hbm,
    out_ref,
    conc,
    vel,
    diff,
    values,
    edges,
    x_rows,
    x_send,
    x_recv,
    z_send,
    z_recv,
    held,
    held_edge,
    send,
    recv,
    ready,
    load_sem,
    z_sem,
    x_send_sem,
    x_recv_sem,
    outer_sem,
    inner_sem,
):
    layers, width, rays = diff.shape
    groups = width // ROWS
    own = rays // n
    per_tile = LANES // own
    total = layers * n
    half = 0.5 * ADVECT
    bright = math.sqrt(total)
    me = lax.axis_index("depth")
    lane_block = lax.axis_index("tile")
    left, right = lane_block == 0, lane_block == tiles - 1
    before_tile = lax.rem(lane_block + tiles - 1, tiles)
    after_tile = lax.rem(lane_block + 1, tiles)
    parity = lax.rem(me, 2)
    odd = parity == 1
    sibling = me + 1 - 2 * parity
    z_outer = parity * (layers - 1)
    z_inner = (1 - parity) * (layers - 1)

    barrier = pltpu.get_barrier_semaphore()
    load_conc = pltpu.make_async_copy(
        conc_hbm, conc.at[:, pl.ds(ROWS, width), :], load_sem.at[0]
    )
    load_conc.start()

    rest = pl.ds(1 - parity, layers - 1)
    first_loads = [
        pltpu.make_async_copy(vel_hbm.at[:, z_outer], vel.at[:, z_outer], load_sem.at[1]),
        pltpu.make_async_copy(diff_hbm.at[z_outer], diff.at[z_outer], load_sem.at[2]),
    ]
    last_loads = [
        pltpu.make_async_copy(vel_hbm.at[:, rest], vel.at[:, rest], load_sem.at[3]),
        pltpu.make_async_copy(diff_hbm.at[rest], diff.at[rest], load_sem.at[4]),
    ]
    for load in first_loads:
        load.start()
    for k in range(1, n):
        pl.semaphore_signal(
            barrier, inc=1, device_id={"depth": lax.rem(me + k, n)}, device_id_type=MESH
        )

    for load in last_loads:
        load.start()
    @pl.when(jnp.logical_not(right))
    def _():
        for k in range(n):
            pl.semaphore_signal(barrier, inc=1, device_id=(k, after_tile), device_id_type=MESH)

    zero_rows = jnp.zeros((ROWS, rays), jnp.float32)
    for z in range(layers):
        conc[z, pl.ds(0, ROWS), :] = zero_rows
        conc[z, pl.ds(ROWS + width, ROWS), :] = zero_rows
    x_rows[...] = jnp.zeros_like(x_rows)

    @pl.when(left)
    def _():
        for k in range(n):
            x_recv[k, pl.ds(0, 2), :] = jnp.zeros((2, LANES), jnp.float32)

    @pl.when(right)
    def _():
        for k in range(n):
            x_recv[k, pl.ds(2, 2), :] = jnp.zeros((2, LANES), jnp.float32)

    slot_of = lax.broadcasted_iota(jnp.int32, (ROWS, LANES), 1) // SLOT
    sub = lax.broadcasted_iota(jnp.int32, (ROWS, LANES), 0)

    def pack(piece, store):
        for tile in range(rays // LANES):
            source = [piece(g, pl.ds(tile * LANES, LANES)) for g in range(4)]
            if own == SLOT:
                for j, block in enumerate(transpose_slots(source)):
                    store(tile * per_tile + j, block)
                continue
            for j in range(per_tile):
                block = None
                for g in range(4):
                    shift = (SLOT * g - j * own) % LANES
                    moved = pltpu.roll(source[g], shift, 1) if shift else source[g]
                    block = moved if block is None else jnp.where(slot_of == g, moved, block)
                store(tile * per_tile + j, block)

    def into(ref, *where):
        def store(k, block):
            ref[(k, *where)] = block

        return store

    load_conc.wait()
    for z in range(layers):
        q, r = z % 4, z // 4
        x_rows[q, pl.ds(r, 1), :] = conc[z, pl.ds(ROWS, 1), :]
        x_rows[q, pl.ds(2 + r, 1), :] = conc[z, pl.ds(ROWS + width - 1, 1), :]
    pack(lambda g, lanes: x_rows[g, :, lanes], into(x_send))
    pack(lambda g, lanes: conc[z_inner, pl.ds(ROWS + g * ROWS, ROWS), lanes], into(z_send))

    z_copy = pltpu.make_async_remote_copy(
        src_ref=z_send,
        dst_ref=z_recv,
        send_sem=z_sem.at[0],
        recv_sem=z_sem.at[1],
        device_id={"depth": sibling},
        device_id_type=MESH,
    )
    def to_left(k):
        return pltpu.make_async_remote_copy(
            src_ref=x_send.at[k, pl.ds(0, 2)],
            dst_ref=x_recv.at[me, pl.ds(2, 2)],
            send_sem=x_send_sem.at[0],
            recv_sem=x_recv_sem.at[1],
            device_id=(k, before_tile),
            device_id_type=MESH,
        )

    def to_right(k):
        return pltpu.make_async_remote_copy(
            src_ref=x_send.at[k, pl.ds(2, 2)],
            dst_ref=x_recv.at[me, pl.ds(0, 2)],
            send_sem=x_send_sem.at[1],
            recv_sem=x_recv_sem.at[0],
            device_id=(k, after_tile),
            device_id_type=MESH,
        )

    pack(lambda g, lanes: conc[z_outer, pl.ds(ROWS + g * ROWS, ROWS), lanes], into(send, 2))
    for load in first_loads:
        load.wait()

    lane = lax.broadcasted_iota(jnp.int32, (ROWS, rays), 1)

    def local_update(z, start, sign=None):
        rows = pl.ds(start, ROWS)
        here = conc[z, pl.ds(ROWS + start, ROWS), :]
        left_cells = conc[z, pl.ds(ROWS + start - 1, ROWS), :]
        right_cells = conc[z, pl.ds(ROWS + start + 1, ROWS), :]
        lower_cells = jnp.where(lane == 0, 0.0, pltpu.roll(here, 1, 1))
        upper_cells = jnp.where(lane == rays - 1, 0.0, pltpu.roll(here, rays - 1, 1))
        spread = left_cells + right_cells + lower_cells + upper_cells
        flow = vel[1, z, rows, :] * (right_cells - left_cells) + vel[2, z, rows, :] * (
            upper_cells - lower_cells
        )
        if sign is None:
            back = conc[z - 1, pl.ds(ROWS + start, ROWS), :]
            front = conc[z + 1, pl.ds(ROWS + start, ROWS), :]
            spread = spread + (back + front)
            slope = front - back
        else:
            step, factor = sign
            beside = conc[z + step, pl.ds(ROWS + start, ROWS), :]
            spread = spread + beside
            slope = factor * beside
        flow = flow + vel[0, z, rows, :] * slope
        return here + diff[z, rows, :] * (spread - 6.0 * here) - half * flow

    def shade(mixed):
        bend = jnp.tanh(mixed)
        passed = jnp.exp((bend + 2.0) * (-1.0 / total))
        return bend, passed

    def add_cell(state, mixed):
        bend, passed = shade(mixed)
        if state is None:
            weight = 1.0 - passed
            return weight * mixed, weight * bend, weight * (mixed * mixed - 1.0), passed
        one, two, three, through = state
        weight = through * (1.0 - passed)
        return (
            one + weight * mixed,
            two + weight * bend,
            three + weight * (mixed * mixed - 1.0),
            through * passed,
        )

    toward = jnp.where(odd, -1.0, 1.0)

    def boundary(z, step, factor, v):
        for g in range(groups):
            rows = pl.ds(g * ROWS, ROWS)
            values[v, rows, :] = local_update(z, g * ROWS, (step, factor))
            values[v + 1, rows, :] = diff[z, rows, :] + (half * factor) * vel[0, z, rows, :]

    boundary(z_outer, 1 - 2 * parity, toward, 0)

    def piece_of(v):
        return lambda g, lanes: values[v, pl.ds(g * ROWS, ROWS), lanes]

    for i in range(2):
        pack(piece_of(i), into(send, i))

    def part(target, k, slots, sems):
        return pltpu.make_async_remote_copy(
            src_ref=send.at[target, slots],
            dst_ref=recv.at[k, slots],
            send_sem=sems.at[0],
            recv_sem=sems.at[1],
            device_id={"depth": target},
            device_id_type=MESH,
        )

    outer, inner = pl.ds(0, OUTER), pl.ds(OUTER, INNER)

    def part_to(d, slots, sems):
        @pl.when(me != d)
        def _():
            part(d, lax.rem(d + n - me, n), slots, sems).start()

    def parts_beyond(slots, sems):
        for k in range(1, n):
            target = lax.rem(me + k, n)

            @pl.when(target >= EARLY)
            def _():
                part(target, k, slots, sems).start()

    pl.semaphore_wait(barrier, n - 1 + n * jnp.where(left, 0, 1))
    z_copy.start()
    for d in range(EARLY):
        part_to(d, outer, outer_sem)
    parts_beyond(outer, outer_sem)

    @pl.when(jnp.logical_not(left))
    def _():
        pl.semaphore_signal(ready.at[1], inc=1, device_id=(me, before_tile), device_id_type=MESH)

    @pl.when(jnp.logical_not(left))
    def _():
        for k in range(n):
            to_left(k).start()

    for load in last_loads:
        load.wait()

    boundary(z_inner, 2 * parity - 1, -toward, 2)

    first_row, last_row = pl.ds(0, 1), pl.ds(width - 1, 1)

    def note_gain(z):
        q, r = z % 4, z // 4
        edges[q, pl.ds(4 + r, 1), :] = diff[z, first_row, :] + half * vel[1, z, first_row, :]
        edges[q, pl.ds(6 + r, 1), :] = diff[z, last_row, :] - half * vel[1, z, last_row, :]

    for g in range(groups):
        state = None
        for z in range(1, layers - 1):
            mixed = local_update(z, g * ROWS)
            if g == 0:
                edges[z % 4, pl.ds(z // 4, 1), :] = mixed[:1]
            if g == groups - 1:
                edges[z % 4, pl.ds(2 + z // 4, 1), :] = mixed[ROWS - 1 :]
            state = add_cell(state, mixed)
        for c in range(4):
            values[4 + c, pl.ds(g * ROWS, ROWS), :] = state[c]
    for z in range(layers):
        note_gain(z)
    for e, row in enumerate((first_row, last_row)):
        ends = values[0, row, :], values[2, row, :]
        edges[0, pl.ds(2 * e, 1), :] = jnp.where(odd, ends[1], ends[0])
        edges[3, pl.ds(2 * e + 1, 1), :] = jnp.where(odd, ends[0], ends[1])
    for v in range(6):
        pack(piece_of(2 + v), into(held, v))
    pack(lambda g, lanes: edges[g, :, lanes], into(held_edge))

    def into_edges(change, z):
        if z == 0:
            first, last = change, pltpu.roll(pltpu.roll(change, SLOT, 1), 3, 0)
            where = slot_of == 0, sub == 0, sub == 2
        else:
            first = pltpu.roll(pltpu.roll(change, LANES - SLOT, 1), 1, 0)
            last = pltpu.roll(change, 4, 0)
            where = slot_of == 3, sub == 1, sub == 3
        moved = jnp.where(where[1], first, jnp.where(where[2], last, 0.0))
        return jnp.where(where[0], moved, 0.0)

    z_copy.wait_recv()
    def finish(k):
        change = held[k, 1] * z_recv[k]
        mixed = held[k, 0] + change
        bend, passed = shade(mixed)
        through = held[k, 5]
        weight = 1.0 - passed
        scale = jnp.where(odd, passed, 1.0)
        weight = jnp.where(odd, weight, weight * through)
        for c, term in enumerate((mixed, bend, mixed * mixed - 1.0)):
            send[k, OUTER + c] = scale * held[k, 2 + c] + weight * term
        send[k, OUTER + 3] = through * passed
        packed = held_edge[k] + jnp.where(
            odd, into_edges(change, 0), into_edges(change, layers - 1)
        )
        send[k, OUTER + 4] = jnp.where(odd, pltpu.roll(packed, 4, 0), packed)

    def all_of(slots, sems):
        others = pl.ds(1, n - 1)
        return pltpu.make_async_remote_copy(
            src_ref=send.at[others, slots],
            dst_ref=recv.at[others, slots],
            send_sem=sems.at[0],
            recv_sem=sems.at[1],
            device_id={"depth": sibling},
            device_id_type=MESH,
        )

    for d in range(EARLY):
        finish(d)
    for d in range(EARLY):
        part_to(d, inner, inner_sem)
    for k in range(EARLY, n):
        finish(k)
    parts_beyond(inner, inner_sem)

    @pl.when(jnp.logical_not(right))
    def _():
        pl.semaphore_wait(ready.at[1], 1)
        for k in range(n):
            to_right(k).start()

    recv[0] = send[me]

    def all_edges(side):
        return pltpu.make_async_remote_copy(
            src_ref=x_send.at[:, pl.ds(2 * side, 2)],
            dst_ref=x_recv.at[:, pl.ds(2 * side, 2)],
            send_sem=x_send_sem.at[side],
            recv_sem=x_recv_sem.at[side],
            device_id={"depth": sibling},
            device_id_type=MESH,
        )

    outer_copies, inner_copies = all_of(outer, outer_sem), all_of(inner, inner_sem)
    outer_copies.wait_recv()
    index = [lax.rem(me - s + n, n) for s in range(n)]
    cells = []
    edge_cells = []
    for s in range(n):
        beyond = s - 1 if s % 2 == 0 else s + 1
        mixed = recv[index[s], 0]
        change = None
        if 0 <= beyond < n:
            change = recv[index[s], 1] * recv[index[beyond], 2]
            mixed = mixed + change
            change = into_edges(change, 0 if s % 2 == 0 else layers - 1)
        bend, passed = shade(mixed)
        cells.append((mixed, bend, mixed * mixed - 1.0, passed))
        edge_cells.append(pltpu.roll(change, 4, 0) if s % 2 == 1 and change is not None else change)

    for side, absent in ((0, left), (1, right)):

        @pl.when(jnp.logical_not(absent))
        def _():
            all_edges(side).wait_recv()

    beside_cells = [x_recv[i] if i % 2 == 0 else pltpu.roll(x_recv[i], 4, 0) for i in range(n)]

    inner_copies.wait_recv()
    state = None
    for s in range(n):
        bricks = [None, None]
        *terms, passed = cells[s]
        weight = 1.0 - passed
        bricks[s % 2] = tuple(weight * x for x in terms) + (passed,)
        bricks[1 - s % 2] = tuple(recv[index[s], OUTER + c] for c in range(4))
        for brick in bricks:
            if state is None:
                state = brick
            else:
                through = state[3]
                state = tuple(state[c] + through * brick[c] for c in range(3)) + (
                    through * brick[3],
                )
    picture = [bright * state[c] for c in range(3)] + [1.0 - state[3]]
    for c in range(4):
        for g in range(groups):
            color = pltpu.roll(picture[c], LANES - SLOT * g, 1) if g else picture[c]
            out_ref[c, pl.ds(g * ROWS, ROWS), :] = color[:, :own]

    through = None
    sums = None
    odd_row, low = sub % 2 == 1, sub < 4
    for s in range(0, n, 2):
        two = []
        for i in (s, s + 1):
            packed = recv[index[i], OUTER + 4]
            mixed = packed + pltpu.roll(packed, 4, 0) * beside_cells[i]
            two.append(mixed if edge_cells[i] is None else mixed + edge_cells[i])
        mixed = jnp.where(low, two[0], two[1])
        bend, passed = shade(mixed)
        ahead, four = None, passed
        for q in range(1, 4):
            moved = pltpu.roll(passed, q * SLOT, 1)
            four = four * moved
            moved = jnp.where(slot_of >= q, moved, 1.0)
            ahead = moved if ahead is None else ahead * moved
        by = {q: pltpu.roll(four, q, 0) for q in (1, 3, 4, 5, 7)}
        partner = jnp.where(odd_row, by[1], by[7])
        other = by[4] * jnp.where(odd_row, by[5], by[3])
        ahead = ahead * jnp.where(odd_row, partner, 1.0) * jnp.where(low, 1.0, other)
        eight = four * partner
        if through is not None:
            ahead = ahead * through
        weight = ahead * (1.0 - passed)
        terms = (weight * mixed, weight * bend, weight * (mixed * mixed - 1.0))
        sums = terms if sums is None else tuple(x + y for x, y in zip(sums, terms))
        through = eight * other if through is None else through * (eight * other)
    rows_of = []
    for x in sums:
        x = (x + pltpu.roll(x, SLOT, 1)) + (pltpu.roll(x, 2 * SLOT, 1) + pltpu.roll(x, 3 * SLOT, 1))
        x = (x + pltpu.roll(x, 4, 0)) + (pltpu.roll(x, 3, 0) + pltpu.roll(x, 7, 0))
        rows_of.append(bright * x)
    rows_of.append(1.0 - through)
    for c in range(4):
        out_ref[c, pl.ds(0, 1), :] = rows_of[c][:1, :own]
        out_ref[c, pl.ds(width - 1, 1), :] = rows_of[c][2:3, :own]

    z_copy.wait_send()

    outer_copies.wait_send()
    inner_copies.wait_send()
    for side, absent in ((0, left), (1, right)):

        @pl.when(jnp.logical_not(absent))
        def _():
            all_edges(side).wait_send()


def solution(mesh):
    n, tiles = mesh.shape["depth"], mesh.shape["tile"]

    def body(concentration, velocity, diffusivity):
        layers, width, rays = concentration.shape
        groups = width // ROWS
        own = rays // n
        assert own <= SLOT and LANES % own == 0 and layers == ROWS and groups == 4 and n % 2 == 0

        def block(*shape):
            return pltpu.VMEM(shape, jnp.float32)

        scratch = [
            block(layers, width + 2 * ROWS, rays),
            block(*velocity.shape),
            block(*diffusivity.shape),
            block(8, width, rays),
            block(4, ROWS, rays),
            block(4, ROWS, rays),
            block(n, ROWS, LANES),
            block(n, ROWS, LANES),
            block(n, ROWS, LANES),
            block(n, ROWS, LANES),
            block(n, 6, ROWS, LANES),
            block(n, ROWS, LANES),
            block(n, OUTER + INNER, ROWS, LANES),
            block(n, OUTER + INNER, ROWS, LANES),
            pltpu.SemaphoreType.REGULAR((2,)),
            pltpu.SemaphoreType.DMA((5,)),
            pltpu.SemaphoreType.DMA((2,)),
            pltpu.SemaphoreType.DMA((2,)),
            pltpu.SemaphoreType.DMA((2,)),
            pltpu.SemaphoreType.DMA((2,)),
            pltpu.SemaphoreType.DMA((2,)),
        ]
        return pl.pallas_call(
            functools.partial(kernel, n, tiles),
            out_shape=jax.ShapeDtypeStruct((4, width, own), jnp.float32),
            in_specs=[pl.BlockSpec(memory_space=pl.ANY)] * 3,
            out_specs=pl.BlockSpec(memory_space=pltpu.VMEM),
            scratch_shapes=scratch,
            compiler_params=pltpu.CompilerParams(collective_id=0, has_side_effects=True, vmem_limit_bytes=16 << 20),
        )(*[pltpu.with_memory_space_constraint(v, pltpu.HBM) for v in (concentration, velocity, diffusivity)])

    return jax.shard_map(
        body,
        mesh=mesh,
        in_specs=(
            P("depth", "tile", None),
            P(None, "depth", "tile", None),
            P("depth", "tile", None),
        ),
        out_specs=P(None, "tile", "depth"),
        check_vma=False,
    )
```

```python
import functools
import math

import jax
import jax.numpy as jnp
from jax import lax
from jax.experimental import pallas as pl
from jax.experimental.pallas import tpu as pltpu
from jax.sharding import PartitionSpec as P

ADVECT = 0.25
LANES = 128
ROWS = 8
SLOT = LANES // 4
MESH = pl.DeviceIdType.MESH
OUTER, INNER = 3, 5
EARLY = 2


def transpose_slots(tiles):
    slot = lax.broadcasted_iota(jnp.int32, (ROWS, LANES), 1) // SLOT
    a, b, c, d = tiles
    odd, high = slot % 2 == 1, slot >= 2

    def swap(x, y, step, mask):
        return (
            jnp.where(mask, pltpu.roll(y, step, 1), x),
            jnp.where(mask, y, pltpu.roll(x, LANES - step, 1)),
        )

    a, b = swap(a, b, SLOT, odd)
    c, d = swap(c, d, SLOT, odd)
    a, c = swap(a, c, 2 * SLOT, high)
    b, d = swap(b, d, 2 * SLOT, high)
    return a, b, c, d


def kernel(
    n,
    tiles,
    conc_hbm,
    vel_hbm,
    diff_hbm,
    out_ref,
    conc,
    vel,
    diff,
    values,
    edges,
    x_rows,
    x_send,
    x_recv,
    x_none,
    z_send,
    z_recv,
    held,
    held_edge,
    send,
    recv,
    ready,
    load_sem,
    z_sem,
    x_send_sem,
    x_recv_sem,
    outer_sem,
    inner_sem,
):
    layers, width, rays = diff.shape
    groups = width // ROWS
    own = rays // n
    per_tile = LANES // own
    total = layers * n
    half = 0.5 * ADVECT
    bright = math.sqrt(total)
    me = lax.axis_index("depth")
    lane_block = lax.axis_index("tile")
    left, right = lane_block == 0, lane_block == tiles - 1
    before_tile = lax.rem(lane_block + tiles - 1, tiles)
    after_tile = lax.rem(lane_block + 1, tiles)
    parity = lax.rem(me, 2)
    odd = parity == 1
    sibling = me + 1 - 2 * parity
    z_outer = parity * (layers - 1)
    z_inner = (1 - parity) * (layers - 1)

    barrier = pltpu.get_barrier_semaphore()
    load_conc = pltpu.make_async_copy(
        conc_hbm, conc.at[:, pl.ds(ROWS, width), :], load_sem.at[0]
    )
    load_conc.start()

    rest = pl.ds(1 - parity, layers - 1)
    first_loads = [
        pltpu.make_async_copy(vel_hbm.at[:, z_outer], vel.at[:, z_outer], load_sem.at[1]),
        pltpu.make_async_copy(diff_hbm.at[z_outer], diff.at[z_outer], load_sem.at[2]),
    ]
    last_loads = [
        pltpu.make_async_copy(vel_hbm.at[:, rest], vel.at[:, rest], load_sem.at[3]),
        pltpu.make_async_copy(diff_hbm.at[rest], diff.at[rest], load_sem.at[4]),
    ]
    for load in first_loads:
        load.start()
    for k in range(1, n):
        pl.semaphore_signal(
            barrier, inc=1, device_id={"depth": lax.rem(me + k, n)}, device_id_type=MESH
        )

    for load in last_loads:
        load.start()
    @pl.when(jnp.logical_not(right))
    def _():
        for k in range(n):
            pl.semaphore_signal(barrier, inc=1, device_id=(k, after_tile), device_id_type=MESH)

    zero_rows = jnp.zeros((ROWS, rays), jnp.float32)
    for z in range(layers):
        conc[z, pl.ds(0, ROWS), :] = zero_rows
        conc[z, pl.ds(ROWS + width, ROWS), :] = zero_rows
    x_rows[...] = jnp.zeros_like(x_rows)

    x_none[...] = jnp.zeros_like(x_none)
    for side, absent in ((0, left), (1, right)):

        @pl.when(absent)
        def _():
            pltpu.make_async_copy(
                x_none, x_recv.at[:, pl.ds(2 * side, 2)], x_recv_sem.at[side]
            ).start()

    slot_of = lax.broadcasted_iota(jnp.int32, (ROWS, LANES), 1) // SLOT
    sub = lax.broadcasted_iota(jnp.int32, (ROWS, LANES), 0)

    def pack(piece, store):
        for tile in range(rays // LANES):
            source = [piece(g, pl.ds(tile * LANES, LANES)) for g in range(4)]
            if own == SLOT:
                for j, block in enumerate(transpose_slots(source)):
                    store(tile * per_tile + j, block)
                continue
            for j in range(per_tile):
                block = None
                for g in range(4):
                    shift = (SLOT * g - j * own) % LANES
                    moved = pltpu.roll(source[g], shift, 1) if shift else source[g]
                    block = moved if block is None else jnp.where(slot_of == g, moved, block)
                store(tile * per_tile + j, block)

    def into(ref, *where):
        def store(k, block):
            ref[(k, *where)] = block

        return store

    load_conc.wait()
    for z in range(layers):
        q, r = z % 4, z // 4
        x_rows[q, pl.ds(r, 1), :] = conc[z, pl.ds(ROWS, 1), :]
        x_rows[q, pl.ds(2 + r, 1), :] = conc[z, pl.ds(ROWS + width - 1, 1), :]
    pack(lambda g, lanes: x_rows[g, :, lanes], into(x_send))
    pack(lambda g, lanes: conc[z_inner, pl.ds(ROWS + g * ROWS, ROWS), lanes], into(z_send))

    z_copy = pltpu.make_async_remote_copy(
        src_ref=z_send,
        dst_ref=z_recv,
        send_sem=z_sem.at[0],
        recv_sem=z_sem.at[1],
        device_id={"depth": sibling},
        device_id_type=MESH,
    )
    def to_left(k):
        return pltpu.make_async_remote_copy(
            src_ref=x_send.at[k, pl.ds(0, 2)],
            dst_ref=x_recv.at[me, pl.ds(2, 2)],
            send_sem=x_send_sem.at[0],
            recv_sem=x_recv_sem.at[1],
            device_id=(k, before_tile),
            device_id_type=MESH,
        )

    def to_right(k):
        return pltpu.make_async_remote_copy(
            src_ref=x_send.at[k, pl.ds(2, 2)],
            dst_ref=x_recv.at[me, pl.ds(0, 2)],
            send_sem=x_send_sem.at[1],
            recv_sem=x_recv_sem.at[0],
            device_id=(k, after_tile),
            device_id_type=MESH,
        )

    pack(lambda g, lanes: conc[z_outer, pl.ds(ROWS + g * ROWS, ROWS), lanes], into(send, 2))
    for load in first_loads:
        load.wait()

    lane = lax.broadcasted_iota(jnp.int32, (ROWS, rays), 1)

    def local_update(z, start, sign=None):
        rows = pl.ds(start, ROWS)
        here = conc[z, pl.ds(ROWS + start, ROWS), :]
        left_cells = conc[z, pl.ds(ROWS + start - 1, ROWS), :]
        right_cells = conc[z, pl.ds(ROWS + start + 1, ROWS), :]
        lower_cells = jnp.where(lane == 0, 0.0, pltpu.roll(here, 1, 1))
        upper_cells = jnp.where(lane == rays - 1, 0.0, pltpu.roll(here, rays - 1, 1))
        spread = left_cells + right_cells + lower_cells + upper_cells
        flow = vel[1, z, rows, :] * (right_cells - left_cells) + vel[2, z, rows, :] * (
            upper_cells - lower_cells
        )
        if sign is None:
            back = conc[z - 1, pl.ds(ROWS + start, ROWS), :]
            front = conc[z + 1, pl.ds(ROWS + start, ROWS), :]
            spread = spread + (back + front)
            slope = front - back
        else:
            step, factor = sign
            beside = conc[z + step, pl.ds(ROWS + start, ROWS), :]
            spread = spread + beside
            slope = factor * beside
        flow = flow + vel[0, z, rows, :] * slope
        return here + diff[z, rows, :] * (spread - 6.0 * here) - half * flow

    def shade(mixed):
        bend = jnp.tanh(mixed)
        passed = jnp.exp((bend + 2.0) * (-1.0 / total))
        return bend, passed

    def add_cell(state, mixed):
        bend, passed = shade(mixed)
        if state is None:
            weight = 1.0 - passed
            return weight * mixed, weight * bend, weight * (mixed * mixed - 1.0), passed
        one, two, three, through = state
        weight = through * (1.0 - passed)
        return (
            one + weight * mixed,
            two + weight * bend,
            three + weight * (mixed * mixed - 1.0),
            through * passed,
        )

    toward = jnp.where(odd, -1.0, 1.0)

    def boundary(z, step, factor, v):
        for g in range(groups):
            rows = pl.ds(g * ROWS, ROWS)
            values[v, rows, :] = local_update(z, g * ROWS, (step, factor))
            values[v + 1, rows, :] = diff[z, rows, :] + (half * factor) * vel[0, z, rows, :]

    boundary(z_outer, 1 - 2 * parity, toward, 0)

    def piece_of(v):
        return lambda g, lanes: values[v, pl.ds(g * ROWS, ROWS), lanes]

    for i in range(2):
        pack(piece_of(i), into(send, i))

    def part(target, k, slots, sems):
        return pltpu.make_async_remote_copy(
            src_ref=send.at[target, slots],
            dst_ref=recv.at[k, slots],
            send_sem=sems.at[0],
            recv_sem=sems.at[1],
            device_id={"depth": target},
            device_id_type=MESH,
        )

    outer, inner = pl.ds(0, OUTER), pl.ds(OUTER, INNER)

    others = [jnp.where(i < me, i, i + 1) for i in range(n - 1)]

    def parts(targets, slots, sems):
        for target in targets:
            part(target, lax.rem(target + n - me, n), slots, sems).start()

    pl.semaphore_wait(barrier, n - 1 + n * jnp.where(left, 0, 1))
    parts(others[:EARLY], outer, outer_sem)
    z_copy.start()
    parts(others[EARLY:], outer, outer_sem)

    @pl.when(jnp.logical_not(left))
    def _():
        pl.semaphore_signal(ready.at[1], inc=1, device_id=(me, before_tile), device_id_type=MESH)

    @pl.when(jnp.logical_not(left))
    def _():
        for k in range(n):
            to_left(k).start()

    for load in last_loads:
        load.wait()

    boundary(z_inner, 2 * parity - 1, -toward, 2)

    first_row, last_row = pl.ds(0, 1), pl.ds(width - 1, 1)

    def note_gain(z):
        q, r = z % 4, z // 4
        edges[q, pl.ds(4 + r, 1), :] = diff[z, first_row, :] + half * vel[1, z, first_row, :]
        edges[q, pl.ds(6 + r, 1), :] = diff[z, last_row, :] - half * vel[1, z, last_row, :]

    for g in range(groups):
        state = None
        for z in range(1, layers - 1):
            mixed = local_update(z, g * ROWS)
            if g == 0:
                edges[z % 4, pl.ds(z // 4, 1), :] = mixed[:1]
            if g == groups - 1:
                edges[z % 4, pl.ds(2 + z // 4, 1), :] = mixed[ROWS - 1 :]
            state = add_cell(state, mixed)
        for c in range(4):
            values[4 + c, pl.ds(g * ROWS, ROWS), :] = state[c]
    for z in range(layers):
        note_gain(z)
    for e, row in enumerate((first_row, last_row)):
        ends = values[0, row, :], values[2, row, :]
        edges[0, pl.ds(2 * e, 1), :] = jnp.where(odd, ends[1], ends[0])
        edges[3, pl.ds(2 * e + 1, 1), :] = jnp.where(odd, ends[0], ends[1])
    for v in range(6):
        pack(piece_of(2 + v), into(held, v))
    pack(lambda g, lanes: edges[g, :, lanes], into(held_edge))

    def into_edges(change, z):
        if z == 0:
            first, last = change, pltpu.roll(pltpu.roll(change, SLOT, 1), 3, 0)
            where = slot_of == 0, sub == 0, sub == 2
        else:
            first = pltpu.roll(pltpu.roll(change, LANES - SLOT, 1), 1, 0)
            last = pltpu.roll(change, 4, 0)
            where = slot_of == 3, sub == 1, sub == 3
        moved = jnp.where(where[1], first, jnp.where(where[2], last, 0.0))
        return jnp.where(where[0], moved, 0.0)

    z_copy.wait_recv()
    def finish(k):
        change = held[k, 1] * z_recv[k]
        mixed = held[k, 0] + change
        bend, passed = shade(mixed)
        through = held[k, 5]
        weight = 1.0 - passed
        scale = jnp.where(odd, passed, 1.0)
        weight = jnp.where(odd, weight, weight * through)
        for c, term in enumerate((mixed, bend, mixed * mixed - 1.0)):
            send[k, OUTER + c] = scale * held[k, 2 + c] + weight * term
        send[k, OUTER + 3] = through * passed
        packed = held_edge[k] + jnp.where(
            odd, into_edges(change, 0), into_edges(change, layers - 1)
        )
        send[k, OUTER + 4] = jnp.where(odd, pltpu.roll(packed, 4, 0), packed)

    def all_of(slots, sems):
        beside = pl.ds(1, n - 1)
        return pltpu.make_async_remote_copy(
            src_ref=send.at[beside, slots],
            dst_ref=recv.at[beside, slots],
            send_sem=sems.at[0],
            recv_sem=sems.at[1],
            device_id={"depth": sibling},
            device_id_type=MESH,
        )

    for k in range(EARLY + 1):
        finish(k)
    parts(others[:EARLY], inner, inner_sem)
    for k in range(EARLY + 1, n):
        finish(k)
    parts(others[EARLY:], inner, inner_sem)

    @pl.when(jnp.logical_not(right))
    def _():
        pl.semaphore_wait(ready.at[1], 1)
        for k in range(n):
            to_right(k).start()

    recv[0] = send[me]

    def all_edges(side):
        return pltpu.make_async_remote_copy(
            src_ref=x_send.at[:, pl.ds(2 * side, 2)],
            dst_ref=x_recv.at[:, pl.ds(2 * side, 2)],
            send_sem=x_send_sem.at[side],
            recv_sem=x_recv_sem.at[side],
            device_id={"depth": sibling},
            device_id_type=MESH,
        )

    outer_copies, inner_copies = all_of(outer, outer_sem), all_of(inner, inner_sem)
    outer_copies.wait_recv()
    index = [lax.rem(me - s + n, n) for s in range(n)]
    cells = []
    edge_cells = []
    for s in range(n):
        beyond = s - 1 if s % 2 == 0 else s + 1
        mixed = recv[index[s], 0]
        change = None
        if 0 <= beyond < n:
            change = recv[index[s], 1] * recv[index[beyond], 2]
            mixed = mixed + change
            change = into_edges(change, 0 if s % 2 == 0 else layers - 1)
        bend, passed = shade(mixed)
        cells.append((mixed, bend, mixed * mixed - 1.0, passed))
        edge_cells.append(pltpu.roll(change, 4, 0) if s % 2 == 1 and change is not None else change)

    for side in range(2):
        all_edges(side).wait_recv()

    beside_cells = [x_recv[i] if i % 2 == 0 else pltpu.roll(x_recv[i], 4, 0) for i in range(n)]

    inner_copies.wait_recv()
    state = None
    for s in range(n):
        bricks = [None, None]
        *terms, passed = cells[s]
        weight = 1.0 - passed
        bricks[s % 2] = tuple(weight * x for x in terms) + (passed,)
        bricks[1 - s % 2] = tuple(recv[index[s], OUTER + c] for c in range(4))
        for brick in bricks:
            if state is None:
                state = brick
            else:
                through = state[3]
                state = tuple(state[c] + through * brick[c] for c in range(3)) + (
                    through * brick[3],
                )
    picture = [bright * state[c] for c in range(3)] + [1.0 - state[3]]
    for c in range(4):
        for g in range(groups):
            color = pltpu.roll(picture[c], LANES - SLOT * g, 1) if g else picture[c]
            out_ref[c, pl.ds(g * ROWS, ROWS), :] = color[:, :own]

    through = None
    sums = None
    odd_row, low = sub % 2 == 1, sub < 4
    for s in range(0, n, 2):
        two = []
        for i in (s, s + 1):
            packed = recv[index[i], OUTER + 4]
            mixed = packed + pltpu.roll(packed, 4, 0) * beside_cells[i]
            two.append(mixed if edge_cells[i] is None else mixed + edge_cells[i])
        mixed = jnp.where(low, two[0], two[1])
        bend, passed = shade(mixed)
        ahead, four = None, passed
        for q in range(1, 4):
            moved = pltpu.roll(passed, q * SLOT, 1)
            four = four * moved
            moved = jnp.where(slot_of >= q, moved, 1.0)
            ahead = moved if ahead is None else ahead * moved
        by = {q: pltpu.roll(four, q, 0) for q in (1, 3, 4, 5, 7)}
        partner = jnp.where(odd_row, by[1], by[7])
        other = by[4] * jnp.where(odd_row, by[5], by[3])
        ahead = ahead * jnp.where(odd_row, partner, 1.0) * jnp.where(low, 1.0, other)
        eight = four * partner
        if through is not None:
            ahead = ahead * through
        weight = ahead * (1.0 - passed)
        terms = (weight * mixed, weight * bend, weight * (mixed * mixed - 1.0))
        sums = terms if sums is None else tuple(x + y for x, y in zip(sums, terms))
        through = eight * other if through is None else through * (eight * other)
    rows_of = []
    for x in sums:
        x = (x + pltpu.roll(x, SLOT, 1)) + (pltpu.roll(x, 2 * SLOT, 1) + pltpu.roll(x, 3 * SLOT, 1))
        x = (x + pltpu.roll(x, 4, 0)) + (pltpu.roll(x, 3, 0) + pltpu.roll(x, 7, 0))
        rows_of.append(bright * x)
    rows_of.append(1.0 - through)
    for c in range(4):
        out_ref[c, pl.ds(0, 1), :] = rows_of[c][:1, :own]
        out_ref[c, pl.ds(width - 1, 1), :] = rows_of[c][2:3, :own]

    z_copy.wait_send()

    outer_copies.wait_send()
    inner_copies.wait_send()
    for side, absent in ((0, left), (1, right)):

        @pl.when(jnp.logical_not(absent))
        def _():
            all_edges(side).wait_send()


def solution(mesh):
    n, tiles = mesh.shape["depth"], mesh.shape["tile"]

    def body(concentration, velocity, diffusivity):
        layers, width, rays = concentration.shape
        groups = width // ROWS
        own = rays // n
        assert own <= SLOT and LANES % own == 0 and layers == ROWS and groups == 4 and n % 2 == 0

        def block(*shape):
            return pltpu.VMEM(shape, jnp.float32)

        scratch = [
            block(layers, width + 2 * ROWS, rays),
            block(*velocity.shape),
            block(*diffusivity.shape),
            block(8, width, rays),
            block(4, ROWS, rays),
            block(4, ROWS, rays),
            block(n, ROWS, LANES),
            block(n, ROWS, LANES),
            block(n, 2, LANES),
            block(n, ROWS, LANES),
            block(n, ROWS, LANES),
            block(n, 6, ROWS, LANES),
            block(n, ROWS, LANES),
            block(n, OUTER + INNER, ROWS, LANES),
            block(n, OUTER + INNER, ROWS, LANES),
            pltpu.SemaphoreType.REGULAR((2,)),
            pltpu.SemaphoreType.DMA((5,)),
            pltpu.SemaphoreType.DMA((2,)),
            pltpu.SemaphoreType.DMA((2,)),
            pltpu.SemaphoreType.DMA((2,)),
            pltpu.SemaphoreType.DMA((2,)),
            pltpu.SemaphoreType.DMA((2,)),
        ]
        return pl.pallas_call(
            functools.partial(kernel, n, tiles),
            out_shape=jax.ShapeDtypeStruct((4, width, own), jnp.float32),
            in_specs=[pl.BlockSpec(memory_space=pl.ANY)] * 3,
            out_specs=pl.BlockSpec(memory_space=pltpu.VMEM),
            scratch_shapes=scratch,
            compiler_params=pltpu.CompilerParams(collective_id=0, has_side_effects=True, vmem_limit_bytes=16 << 20),
        )(*[pltpu.with_memory_space_constraint(v, pltpu.HBM) for v in (concentration, velocity, diffusivity)])

    return jax.shard_map(
        body,
        mesh=mesh,
        in_specs=(
            P("depth", "tile", None),
            P(None, "depth", "tile", None),
            P("depth", "tile", None),
        ),
        out_specs=P(None, "tile", "depth"),
        check_vma=False,
    )
```
